512 devices in a mesh: patch: 64 (over y, z), visit: 8 (over x, core).
Axes of the slice: x: 4, y: 8, z: 8, core: 2. Of those that a mesh axis runs over, the one named last changes fastest.
Arguments:
- stamps: bfloat16 [8, 8192, 32, 128], P('visit', 'patch'), may hold values from -6 to 6
- coefs: bfloat16 [8, 8192, 64], P('visit', 'patch'), may hold values from -0.75 to 0.75
- basis: bfloat16 [8, 64, 21, 21], P('visit', 'patch'), may hold values from -0.29882812 to 0.29882812
- taps: bfloat16 [8, 8192, 8], P('visit', 'patch'), may hold values from 0.049804688 to 0.59765625
- weights: bfloat16 [8, 8192], P('visit', 'patch'), may hold values from 0.19921875 to 5
- target: int32 [8, 8192, 1], P('visit', 'patch'), may hold values from 0 to 63; in each aligned block of 128 rows (0 to 127, 128 to 255, ..., all dimensions but the last counted through in order) at most 4 rows name the same one
- row_offset: int32 [8, 8192], P('visit', 'patch'), may hold values from 0 to 223
- col_offset: int32 [8, 8192], P('visit', 'patch'), may hold values from 0 to 127
Outputs:
- coadd: float32 [64, 256, 256], P('patch', 'visit')
- depth_map: float32 [64, 256, 256], P('patch', 'visit')
The draws below stay inside these ranges and needn't reach their ends.
Inputs may be any that keep to these rules, and one draw needn't show every extreme that they name: `target`: among the rows of one device no patch is named more than 4 times, a bound that some block reaches.
All inputs are finite; a program needn't handle non-finite values.
Results may differ from the reference program's by a relative error of at most 0.0057.
Values may be sent and summed in bfloat16 or wider, within the bound.
No kernel may reach another device: no remote copies, remote signals or barrier semaphores. Data moves between devices by JAX's collectives and lax.ppermute only.
A program may use at most 64 MiB of HBM per device.

```python
import math
import jax
import jax.numpy as jnp
import numpy as np
from jax import lax

KERNEL = 21
TERMS = 64
STAMP_ROWS = 32
STAMP_COLS = 128
PATCH_ROWS = 256
PATCH_COLS = 256
STAMPS_DEV = 128
PATCHES = 64
VISITS = 8
STAMPS = 8192
CAP = 4


def plant(array, rng, low, largest):
    shape = array.shape
    place = [jax.random.randint(jax.random.fold_in(rng, axis), (), 0, shape[axis]) for axis in range(len(shape))]
    array = array.at[tuple(place)].set(low)
    longest = shape.index(max(shape))
    place[longest] = (place[longest] + 1) % shape[longest]
    return array.at[tuple(place)].set(largest)


def level_of(key, extent, shards, low, largest):
    factor_of = 1.0
    for axis_at, shards_of in shards:
        heights = jax.random.uniform(jax.random.fold_in(jax.random.fold_in(key, 6), axis_at), (shards_of,), jnp.float32, low / len(shards), largest / len(shards))
        factor_of = factor_of * jnp.repeat(jnp.exp(heights), extent[axis_at] // shards_of).reshape((-1,) + (1,) * (len(extent) - 1 - axis_at))
    return factor_of


def shared_out(own_key, own, number, rows, count, top, bound, slope):
    order = jax.random.permutation(own_key, count)
    packed, common = shares(count, rows * top, bound, slope, True), shares(count, rows * top, bound, slope, False)
    places = jnp.arange(count)

    def named(tallies, rotation):
        used = int((tallies > 0).sum())
        fixed = max(1, used // 4)
        passed = fixed + (places - fixed + rotation * (used - fixed)) % max(1, count - fixed)
        return jnp.zeros((count,), jnp.int32).at[order[jnp.where(places < fixed, places, passed)]].set(jnp.asarray(tallies, jnp.int32))

    tallies = jnp.where(number % 4 == 0, named(packed, number // 4), named(common, number - number // 4 - 1))
    mixed = jax.random.permutation(jax.random.fold_in(own, 3), count)
    giver, sink = mixed[0:count // 2 * 2:2], mixed[1:count // 2 * 2:2]
    margin = jnp.minimum(tallies[giver] - 1, bound - tallies[sink]) // 2
    margin = jnp.where((giver == order[0]) | (sink == order[0]) | (tallies[sink] == 0), 0, jnp.maximum(margin, 0))
    passed = jax.random.randint(jax.random.fold_in(own, 4), (count // 2,), 0, 1 << 20) % (margin + 1)
    tallies = tallies.at[giver].add(-passed).at[sink].add(passed)
    labels = jnp.searchsorted(jnp.cumsum(tallies), jnp.arange(rows * top), side="right").astype(jnp.int32)
    table = labels.reshape(top, rows).T
    table = table[jax.random.permutation(jax.random.fold_in(own, 1), rows)]
    rotation = jax.random.randint(jax.random.fold_in(own, 2), (rows, 1), 0, top)
    return jnp.take_along_axis(table, (jnp.arange(top)[None, :] + rotation) % top, axis=1)


def shares(number_of, total, bound, skew, full):
    weights = [(1 << 20) // math.isqrt(rank ** skew) + 1 for rank in range(1, number_of + 1)]
    largest = bound if full else min(bound, max(-(-total // number_of), total * weights[0] // sum(weights)))
    least = 1 if total - largest >= number_of - 1 else 0
    given, surplus = [largest] + [least] * (number_of - 1), total - largest - least * (number_of - 1)
    while surplus > 0:
        candidates = [i for i in range(1, number_of) if given[i] < largest] or [i for i in range(1, number_of) if given[i] < bound]
        whole, left = sum([weights[i] for i in candidates]), surplus
        for i in candidates:
            addition = min(bound - given[i], max(1, left * weights[i] // whole), surplus)
            given[i] = given[i] + addition
            surplus = surplus - addition
    return np.array(given)


def bell_draw(key, dims, scale, limit, split=(), kind=jnp.bfloat16):
    entries = scale * jax.random.normal(key, dims, jnp.float32)
    if split:
        entries = entries * level_of(key, dims, split, -0.22, 0.18)
    return jnp.clip(entries, -limit, limit).astype(kind)


def setup_inputs(seed: int = 0) -> dict:
    arg_keys = jax.random.split(jax.random.key(seed), 9)
    stamps = bell_draw(arg_keys[0], (VISITS, STAMPS, STAMP_ROWS, STAMP_COLS), 1.0, 6.0, ((0, 8), (1, 64)))
    coefs = bell_draw(arg_keys[1], (VISITS, STAMPS, TERMS), 0.125, 0.75, ((0, 8), (1, 64)))
    basis = bell_draw(arg_keys[2], (VISITS, TERMS, KERNEL, KERNEL), 0.048, 0.29882812, ((0, 8), (1, 64)))
    taps = jnp.clip(0.049804688 + 0.54785156 * jax.random.uniform(arg_keys[3], (VISITS, STAMPS, 8), jnp.float32) ** level_of(arg_keys[3], (VISITS, STAMPS, 8), ((0, 8), (1, 64)), -0.2, 0.2), 0.049804688, 0.59765625).astype(jnp.bfloat16)
    weights = jnp.clip(jnp.exp(math.log(5.0) - 3.2227897 * jax.random.uniform(arg_keys[4], (VISITS, STAMPS), jnp.float32) ** level_of(arg_keys[4], (VISITS, STAMPS), ((0, 8), (1, 64)), -0.2, 0.2)), 0.19921875, 5.0).astype(jnp.bfloat16)
    target_keys = jax.random.split(jax.random.fold_in(arg_keys[5], 1), VISITS * STAMPS // STAMPS_DEV)
    target_turns = jax.random.permutation(jax.random.fold_in(arg_keys[5], 3), VISITS * STAMPS // STAMPS_DEV)
    target = jax.vmap(lambda own, number: shared_out(jax.random.fold_in(arg_keys[5], 2), own, number, STAMPS_DEV, PATCHES, 1, CAP, 2))(target_keys, target_turns).reshape((VISITS, STAMPS, 1))
    row_offset = plant(jax.random.randint(arg_keys[6], (VISITS, STAMPS), 0, PATCH_ROWS - STAMP_ROWS), jax.random.fold_in(arg_keys[6], 1), 0, (PATCH_ROWS - STAMP_ROWS) - 1).astype(jnp.int32)
    col_offset = plant(jax.random.randint(arg_keys[7], (VISITS, STAMPS), 0, PATCH_COLS - STAMP_COLS), jax.random.fold_in(arg_keys[7], 1), 0, (PATCH_COLS - STAMP_COLS) - 1).astype(jnp.int32)
    return {"stamps": stamps, "coefs": coefs, "basis": basis, "taps": taps, "weights": weights, "target": target, "row_offset": row_offset, "col_offset": col_offset}


def make_kernels(coefficients, basis_set):
    term_count = basis_set.shape[0]
    kernel_size = basis_set.shape[1]
    flat = jnp.dot(coefficients, basis_set.reshape(term_count, kernel_size * kernel_size), preferred_element_type=jnp.float32)
    return flat.astype(jnp.bfloat16).reshape(coefficients.shape[0], kernel_size, kernel_size)


def convolve(pixels, kernels):
    kernel_size = kernels.shape[1]
    kernel_reach = kernel_size // 2
    height = pixels.shape[1]
    breadth = pixels.shape[2]
    padded = jnp.pad(pixels, ((0, 0), (0, 0), (kernel_reach, kernel_reach)))
    shifted = jnp.stack([padded[:, :, column_shift:column_shift + breadth] for column_shift in range(kernel_size)], axis=1)
    offsets = jnp.arange(height, dtype=jnp.int32)[None, :] - jnp.arange(height, dtype=jnp.int32)[:, None] + kernel_reach
    onehot = (offsets[None, :, :] == jnp.arange(kernel_size, dtype=jnp.int32)[:, None, None]).astype(jnp.float32)
    toeplitz = jnp.einsum("nab,aij->nbij", kernels.astype(jnp.float32), onehot).astype(jnp.bfloat16)
    result = jnp.einsum("nbik,nbkj->nij", toeplitz.astype(jnp.float32), shifted.astype(jnp.float32))
    return result.astype(jnp.bfloat16)


def resample(convolved, tap_values, scale, row_start, col_start):
    height = convolved.shape[1]
    breadth = convolved.shape[2]
    column_gap = jnp.arange(PATCH_COLS, dtype=jnp.int32)[None, :, None] - col_start[:, None, None] - jnp.arange(breadth, dtype=jnp.int32)[None, None, :] + 1
    row_gap = jnp.arange(PATCH_ROWS, dtype=jnp.int32)[None, :, None] - row_start[:, None, None] - jnp.arange(height, dtype=jnp.int32)[None, None, :] + 1
    column_sum = jnp.zeros(column_gap.shape, jnp.float32)
    row_sum = jnp.zeros(row_gap.shape, jnp.float32)
    for tap_index in range(4):
        column_sum = column_sum + jnp.where(column_gap == tap_index, tap_values[:, 4 + tap_index].astype(jnp.float32)[:, None, None], 0.0)
        row_sum = row_sum + jnp.where(row_gap == tap_index, tap_values[:, tap_index].astype(jnp.float32)[:, None, None], 0.0)
    column_map = column_sum.astype(jnp.bfloat16)
    row_map = (scale.astype(jnp.float32)[:, None, None] * row_sum).astype(jnp.bfloat16)
    spread = jnp.einsum("nij,ncj->nic", convolved.astype(jnp.float32), column_map.astype(jnp.float32)).astype(jnp.bfloat16)
    return row_map, column_map, spread


def reference(stamps, coefs, basis, taps, weights, target, row_offset, col_offset):
    block_count = VISITS * STAMPS // STAMPS_DEV
    per_visit = STAMPS // STAMPS_DEV
    blocks = (
        stamps.reshape(block_count, STAMPS_DEV, STAMP_ROWS, STAMP_COLS),
        coefs.reshape(block_count, STAMPS_DEV, TERMS),
        taps.reshape(block_count, STAMPS_DEV, 8),
        weights.reshape(block_count, STAMPS_DEV),
        target.reshape(block_count, STAMPS_DEV),
        row_offset.reshape(block_count, STAMPS_DEV),
        col_offset.reshape(block_count, STAMPS_DEV),
        jnp.arange(block_count, dtype=jnp.int32) // per_visit,
    )

    def update(state, block):
        numerator, depth_map = state
        pixels, coefficients, tap_values, scale, destination, row_start, col_start, visit_index = block
        basis_set = lax.dynamic_index_in_dim(basis, visit_index, 0, keepdims=False)
        convolved = convolve(pixels, make_kernels(coefficients, basis_set))
        row_map, column_map, spread = resample(convolved, tap_values, scale, row_start, col_start)
        contribution = jnp.einsum("nri,nic->nrc", row_map.astype(jnp.float32), spread.astype(jnp.float32))
        row_weight = jnp.sum(row_map.astype(jnp.float32), axis=2)
        column_weight = jnp.sum(column_map.astype(jnp.float32), axis=2)
        numerator = numerator.at[destination].add(contribution)
        depth_map = depth_map.at[destination].add(row_weight[:, :, None] * column_weight[:, None, :])
        return (numerator, depth_map), None

    initial = (jnp.zeros((PATCHES, PATCH_ROWS, PATCH_COLS), jnp.float32), jnp.zeros((PATCHES, PATCH_ROWS, PATCH_COLS), jnp.float32))
    final_state, unused = lax.scan(update, initial, blocks)
    numerator, depth_map = final_state
    return numerator / (1.0 + depth_map), depth_map
```

```python
import functools

import jax
import jax.numpy as jnp
from jax import lax
from jax.experimental import pallas as pl
from jax.experimental.pallas import tpu as pltpu
from jax.sharding import PartitionSpec as P

BF16 = jnp.bfloat16
F32 = jnp.float32
KERNEL = 21
REACH = 10
TERMS = 64
HEIGHT = 32
BREADTH = 128
PATCH = 256
CAP = 4
TAIL = 8
BLOCK_ROWS = CAP * HEIGHT + TAIL
INNER = 3
OUTER = 7
ROWS_T = INNER * HEIGHT
GROUP = 8


def iota(shape, axis):
    return lax.broadcasted_iota(jnp.int32, shape, axis)


def dot(a, b):
    return jnp.dot(a, b, preferred_element_type=F32)


def pack_body(places, target_s, target_row, target_col, stamps, aux, out, count):
    stamp_count = stamps.shape[0]
    out[...] = jnp.zeros_like(out)
    across = target_row[...]
    down = target_col[...]
    square = (stamp_count, stamp_count)
    earlier = (down == across) & (iota(square, 0) < iota(square, 1))
    rank = jnp.sum(jnp.where(earlier, 1, 0), axis=0, keepdims=True)
    row = iota((places * TAIL, stamp_count), 0)
    lane = iota((places * TAIL, stamp_count), 1)
    chosen = jnp.where(row == across * TAIL + (TAIL - CAP) + rank, 1.0, 0.0).astype(BF16)
    part = row & (TAIL - 1)
    shared = jnp.where((lane == part) & (part < TAIL - CAP), 1.0, 0.0).astype(BF16)
    tail = dot(chosen, aux[:stamp_count, :]) + dot(shared, aux[stamp_count:, :])
    out[:, CAP * HEIGHT :, :] = tail.reshape(places, TAIL, BREADTH).astype(BF16)

    def clear(d, carry):
        count[d] = 0
        return carry

    lax.fori_loop(0, places, clear, 0)

    def place(s, carry):
        d = target_s[s]
        k = count[d]
        count[d] = k + 1
        out[d, pl.ds(pl.multiple_of(k * HEIGHT, HEIGHT), HEIGHT), :] = stamps[s]
        return carry

    lax.fori_loop(0, stamp_count, place, 0, unroll=4)


def pack(target, stamps, aux, places):
    stamp_count = stamps.shape[0]
    vmem = pl.BlockSpec(memory_space=pltpu.VMEM)
    return pl.pallas_call(
        functools.partial(pack_body, places),
        out_shape=jax.ShapeDtypeStruct((places, BLOCK_ROWS, BREADTH), BF16),
        in_specs=[pl.BlockSpec(memory_space=pltpu.SMEM), vmem, vmem, vmem, vmem],
        out_specs=vmem,
        scratch_shapes=[pltpu.SMEM((places,), jnp.int32)],
        compiler_params=pltpu.CompilerParams(vmem_limit_bytes=40 << 20),
        name="pack",
    )(target, target[None, :], target[:, None], stamps, aux)


def coadd_body(
    sources, blocks, out, tail, meta, spread_basis, toeplitz, expanded, stack, numer, fields, whole, fields_s, whole_s, sem
):
    slots = CAP * sources
    groups = slots // GROUP
    tail[...] = blocks[:, CAP * HEIGHT :, :].astype(F32).reshape(sources * TAIL, BREADTH)
    basis = jnp.concatenate(
        [tail[pl.ds(q, sources, stride=TAIL), :] for q in range(TAIL - CAP)], axis=1
    ).astype(BF16)
    for k in range(CAP):
        meta[pl.ds(k * sources, sources), :] = tail[pl.ds(TAIL - CAP + k, sources, stride=TAIL), :]
    table = meta[...]
    coefs = table[:, :TERMS].astype(BF16)

    flat = iota((4 * BREADTH, 1), 0)
    a = (flat * 3121) >> 16
    b = flat - a * KERNEL
    outer = (b * 11) >> 5
    there = (b - INNER * outer) * PATCH + outer * HEIGHT + a
    there = jnp.where(flat < KERNEL * KERNEL, there, -1)
    moved = jnp.where(iota((4 * BREADTH, INNER * PATCH), 1) == there, 1.0, 0.0).astype(BF16)
    spread_basis[...] = dot(basis, moved)

    across = iota((TERMS, PATCH), 1) & (HEIGHT - 1)
    for inner in range(INNER):

        def widen(i, carry):
            turned = pltpu.roll(
                spread_basis[:, inner * PATCH : (inner + 1) * PATCH],
                lax.rem(i + (PATCH - REACH), PATCH),
                1,
            )
            near = (across - i <= REACH) & (i - across <= REACH)
            rows = dot(coefs, jnp.where(near, turned, 0.0).astype(BF16))
            at = pl.ds(inner * HEIGHT + i, slots, stride=ROWS_T)
            toeplitz[0, at, :] = rows[:, :BREADTH]
            toeplitz[1, at, :] = rows[:, BREADTH:]
            return carry

        lax.fori_loop(0, HEIGHT, widen, 0)

    turned = table.T
    at = TERMS
    weight = turned[at + 8 : at + 9, :]
    row_start = turned[at + 9 : at + 10, :]
    row_taps = [
        (weight * turned[at + k : at + k + 1, :]).astype(BF16).astype(F32) for k in range(4)
    ]
    fields[...] = jnp.concatenate(
        [turned[at + 4 : at + 8, :], turned[at + 10 : at + 11, :], jnp.zeros((3, slots), F32)], axis=0
    )
    whole[...] = fields[...].astype(jnp.int32)
    copies = [
        pltpu.make_async_copy(fields, fields_s, sem.at[0]),
        pltpu.make_async_copy(whole, whole_s, sem.at[1]),
    ]
    for copy in copies:
        copy.start()

    gap = (iota((PATCH, slots), 0) + 1).astype(F32) - row_start
    row_weight = jnp.zeros((PATCH, slots), F32)
    for k in range(4):
        inside = (gap >= k) & (gap < HEIGHT + k)
        row_weight = row_weight + jnp.where(inside, row_taps[k], 0.0)
    gap = (iota((slots, PATCH), 1) + 1).astype(F32) - table[:, at + 10 : at + 11]
    col_weight = jnp.zeros((slots, PATCH), F32)
    for k in range(4):
        inside = (gap >= k) & (gap < BREADTH + k)
        col_weight = col_weight + jnp.where(inside, table[:, at + 4 + k : at + 5 + k], 0.0)
    row_high = row_weight.astype(BF16)
    row_low = (row_weight - row_high.astype(F32)).astype(BF16)
    col_high = col_weight.astype(BF16)
    col_low = (col_weight - col_high.astype(F32)).astype(BF16)
    depth = dot(row_high, col_high) + (dot(row_high, col_low) + dot(row_low, col_high))
    shares = PATCH // HEIGHT
    for v in range(shares):
        out[v, HEIGHT:, :] = depth[v * HEIGHT : (v + 1) * HEIGHT, :].astype(out.dtype)

    rows = jnp.concatenate(row_taps + [row_start, jnp.zeros((11, slots), F32)], axis=0).astype(BF16)
    owner = iota((slots, GROUP * HEIGHT), 0) - (iota((slots, GROUP * HEIGHT), 1) >> 5)

    def repeat(g, carry):
        hot = jnp.where(owner == g * GROUP, 1.0, 0.0).astype(BF16)
        expanded[g] = dot(rows, hot)
        return carry

    lax.fori_loop(0, groups, repeat, 0)
    for copy in copies:
        copy.wait()

    numer[...] = jnp.zeros_like(numer)
    lane = iota((HEIGHT, BREADTH), 1)
    line = iota((8, BREADTH), 1)
    patch_row = (iota((PATCH, GROUP * HEIGHT), 0) + 1).astype(F32)
    in_stamp = (iota((1, GROUP * HEIGHT), 1) & (HEIGHT - 1)).astype(F32)
    nothing = jnp.zeros((HEIGHT, BREADTH), BF16)
    per_cap = sources // GROUP

    def tall(x):
        return jnp.concatenate([x] * (HEIGHT // 8), axis=0)

    def work(g, carry):
        k = g // per_cap
        first = (g - k * per_cap) * GROUP
        for q in range(GROUP):
            s = g * GROUP + q
            pixels = blocks[first + q, pl.ds(pl.multiple_of(k * HEIGHT, HEIGHT), HEIGHT), :].astype(F32)
            low, high = [], []
            for outer in range(OUTER):
                move = REACH - INNER * outer
                moved = pltpu.roll(pixels, move % BREADTH, 1)
                if move > 0:
                    low.append(jnp.where(lane >= move, moved, 0.0).astype(BF16))
                    if move == 1:
                        moved = jnp.where(lane < move, moved, 0.0)
                    high.append(moved.astype(BF16))
                else:
                    low.append(jnp.where(lane < BREADTH + move, moved, 0.0).astype(BF16))
                    high.append(nothing)
            low.append(nothing)
            high.append(nothing)
            shifted = jnp.concatenate(
                [jnp.concatenate(low, axis=0), jnp.concatenate(high, axis=0)], axis=1
            )
            at = pl.ds(pl.multiple_of(s * ROWS_T, 8), ROWS_T)
            left = jnp.concatenate([toeplitz[0, at, :], toeplitz[1, at, :]], axis=1).astype(BF16)
            product = dot(left, shifted)
            total = product[:HEIGHT, :BREADTH]
            for inner in range(1, INNER):
                part = product[inner * HEIGHT : (inner + 1) * HEIGHT, :]
                total = total + jnp.where(
                    lane < BREADTH - inner,
                    pltpu.roll(part[:, :BREADTH], BREADTH - inner, 1),
                    pltpu.roll(part[:, BREADTH:], BREADTH - inner, 1),
                )
            convolved = total.astype(BF16).astype(F32)
            col_start = whole_s[4, s]
            near, far = [], []
            for t in range(4):
                tap = fields_s[t, s]
                near.append(jnp.where(line >= t, tap, 0.0))
                far.append(jnp.where(line < t, tap, 0.0))
            near[0] = jnp.where((line == 0) & (col_start == 0), 0.0, near[0])
            far[3] = jnp.where((line == 2) & (col_start == BREADTH - 1), 0.0, far[3])
            wide_low = tall(near[0]) * convolved
            wide_high = None
            for t in range(1, 4):
                moved = pltpu.roll(convolved, t, 1)
                wide_low = wide_low + tall(near[t]) * moved
                term = tall(far[t]) * moved
                wide_high = term if wide_high is None else wide_high + term
            wide = jnp.concatenate([wide_low, wide_high], axis=1)
            wide = pltpu.roll(wide, lax.rem(col_start + (PATCH - 1), PATCH), 1)
            stack[pl.ds(q * HEIGHT, HEIGHT), :] = wide.astype(BF16)
        taps = expanded[g]
        gap = patch_row - (taps[4:5, :] + in_stamp)
        row_map = jnp.where(gap == 3.0, taps[3:4, :], 0.0)
        for t in (2, 1, 0):
            row_map = jnp.where(gap == float(t), taps[t : t + 1, :], row_map)
        numer[...] += dot(row_map.astype(BF16), stack[...])
        return carry

    lax.fori_loop(0, groups, work, 0)
    for v in range(shares):
        out[v, :HEIGHT, :] = numer[v * HEIGHT : (v + 1) * HEIGHT, :].astype(out.dtype)


def coadd_sums(blocks):
    sources = blocks.shape[0]
    slots = CAP * sources
    vmem = pl.BlockSpec(memory_space=pltpu.VMEM)
    return pl.pallas_call(
        functools.partial(coadd_body, sources),
        out_shape=jax.ShapeDtypeStruct((PATCH // HEIGHT, 2 * HEIGHT, PATCH), BF16),
        in_specs=[vmem],
        out_specs=vmem,
        scratch_shapes=[
            pltpu.VMEM((sources * TAIL, BREADTH), F32),
            pltpu.VMEM((slots, BREADTH), F32),
            pltpu.VMEM((TERMS, INNER * PATCH), F32),
            pltpu.VMEM((2, slots * ROWS_T, BREADTH), F32),
            pltpu.VMEM((slots // GROUP, 16, GROUP * HEIGHT), F32),
            pltpu.VMEM((GROUP * HEIGHT, PATCH), BF16),
            pltpu.VMEM((PATCH, PATCH), F32),
            pltpu.VMEM((8, slots), F32),
            pltpu.VMEM((8, slots), jnp.int32),
            pltpu.SMEM((8, slots), F32),
            pltpu.SMEM((8, slots), jnp.int32),
            pltpu.SemaphoreType.DMA((2,)),
        ],
        compiler_params=pltpu.CompilerParams(vmem_limit_bytes=48 << 20),
        name="coadd",
    )(blocks)


def per_device(stamps, coefs, basis, taps, weights, target, row_offset, col_offset):
    places = lax.axis_size("patch")
    extras = jnp.concatenate(
        [
            coefs[0],
            taps[0],
            weights[0][:, None],
            row_offset[0].astype(BF16)[:, None],
            col_offset[0].astype(BF16)[:, None],
        ],
        axis=1,
    )
    extras = jnp.pad(extras, ((0, 0), (0, BREADTH - extras.shape[1])))
    flat = jnp.pad(basis.reshape(-1), (0, 4 * BREADTH - KERNEL * KERNEL)).reshape(4, BREADTH)
    aux = jnp.concatenate([extras, jnp.pad(flat, ((0, extras.shape[0] - 4), (0, 0)))], axis=0)
    blocks = pack(target[0, :, 0], stamps[0], aux, places)
    blocks = lax.all_to_all(blocks, "patch", split_axis=0, concat_axis=0, tiled=True)
    sums = coadd_sums(blocks)
    sums = lax.all_to_all(sums, "visit", split_axis=0, concat_axis=0, tiled=True)
    total = jnp.sum(sums.astype(F32), axis=0)
    depth_map = total[HEIGHT:]
    coadd = total[:HEIGHT] / (1.0 + depth_map)
    return (coadd[None], depth_map[None])


def solution(mesh):
    placed = (
        P("visit", "patch", None, None),
        P("visit", "patch", None),
        P("visit", "patch", None, None),
        P("visit", "patch", None),
        P("visit", "patch"),
        P("visit", "patch", None),
        P("visit", "patch"),
        P("visit", "patch"),
    )
    return jax.shard_map(
        per_device,
        mesh=mesh,
        in_specs=placed,
        out_specs=(P("patch", "visit", None), P("patch", "visit", None)),
        check_vma=False,
    )
```

```python
import functools

import jax
import jax.numpy as jnp
from jax import lax
from jax.experimental import pallas as pl
from jax.experimental.pallas import tpu as pltpu
from jax.sharding import PartitionSpec as P

BF16 = jnp.bfloat16
F32 = jnp.float32
KERNEL = 21
REACH = 10
TERMS = 64
HEIGHT = 32
BREADTH = 128
PATCH = 256
CAP = 4
TAIL = 8
BLOCK_ROWS = CAP * HEIGHT + TAIL
INNER = 3
OUTER = 7
WINDOW = HEIGHT + 8
GROUP = 8
SIDE = 6


def iota(shape, axis):
    return lax.broadcasted_iota(jnp.int32, shape, axis)


def dot(a, b):
    return jnp.dot(a, b, preferred_element_type=F32)


def pack_body(target_s, target, stamps, coefs, basis, taps, weights, row_offset, col_offset, out, held, count, sem):
    places = out.shape[0]
    stamp_count = held.shape[0]
    fetch = pltpu.make_async_copy(stamps, held, sem)
    fetch.start()
    out[...] = jnp.zeros_like(out)
    across = jnp.broadcast_to(target[...].astype(F32), (stamp_count, stamp_count))
    square = (stamp_count, stamp_count)
    earlier = (across.T == across) & (iota(square, 0) < iota(square, 1))
    rank = jnp.sum(jnp.where(earlier, 1.0, 0.0), axis=0, keepdims=True)
    place = target[...] * TAIL + (TAIL - CAP) + rank.astype(jnp.int32)
    chosen = jnp.where(iota((places * TAIL, stamp_count), 0) == place, 1.0, 0.0).astype(BF16)
    extras = jnp.concatenate(
        [
            coefs[...].astype(F32),
            taps[...].astype(F32),
            weights[...].astype(F32),
            row_offset[...].astype(F32),
            col_offset[...].astype(F32),
            jnp.zeros((BREADTH - TERMS - 11, stamp_count), F32),
        ],
        axis=0,
    )
    tail = lax.dot_general(
        chosen, extras.astype(BF16), (((1,), (1,)), ((), ())), preferred_element_type=F32
    )
    wide = jnp.pad(basis[...].astype(F32), ((0, 24 - KERNEL), (0, BREADTH - KERNEL)))
    seat = iota(wide.shape, 0)
    seat = seat - SIDE * ((seat * 11) >> 6)
    laid = jnp.where(seat == 0, wide, 0.0)
    for r in range(1, SIDE):
        laid = laid + jnp.where(seat == r, pltpu.roll(wide, r * KERNEL, 1), 0.0)
    fold = jnp.where((iota((TAIL, 24), 1) * 11) >> 6 == iota((TAIL, 24), 0), 1.0, 0.0)
    shared = dot(fold.astype(BF16), laid.astype(BF16))
    tail = tail.reshape(places, TAIL, BREADTH) + shared[None]
    out[:, CAP * HEIGHT :, :] = tail.astype(BF16)

    def clear(d, carry):
        count[d] = 0
        return carry

    lax.fori_loop(0, places, clear, 0, unroll=8)
    fetch.wait()

    def put(s, carry):
        d = target_s[s]
        k = count[d]
        count[d] = k + 1
        out[d, pl.ds(pl.multiple_of(k * HEIGHT, HEIGHT), HEIGHT), :] = held[s]
        return carry

    lax.fori_loop(0, stamp_count, put, 0, unroll=4)


def pack(target, stamps, coefs, basis, taps, weights, row_offset, col_offset, places):
    vmem = pl.BlockSpec(memory_space=pltpu.VMEM)
    return pl.pallas_call(
        pack_body,
        out_shape=jax.ShapeDtypeStruct((places, BLOCK_ROWS, BREADTH), BF16),
        in_specs=[pl.BlockSpec(memory_space=pltpu.SMEM), vmem, pl.BlockSpec(memory_space=pl.ANY)] + [vmem] * 6,
        out_specs=vmem,
        scratch_shapes=[
            pltpu.VMEM(stamps.shape, BF16),
            pltpu.SMEM((places,), jnp.int32),
            pltpu.SemaphoreType.DMA,
        ],
        compiler_params=pltpu.CompilerParams(vmem_limit_bytes=40 << 20),
        name="pack",
    )(target[0], target, stamps, coefs, basis, taps, weights, row_offset, col_offset)


def coadd_body(sources, blocks, out, tail, meta, kernels, padded, numer, fields, whole, fields_s, whole_s, sem):
    slots = CAP * sources
    groups = slots // GROUP
    tail[...] = blocks[:, CAP * HEIGHT :, :].astype(F32).reshape(sources * TAIL, BREADTH)
    basis = jnp.concatenate(
        [tail[pl.ds(q, sources, stride=TAIL), :] for q in range(TAIL - CAP)], axis=1
    ).astype(BF16)
    for k in range(CAP):
        meta[pl.ds(k * sources, sources), :] = tail[pl.ds(TAIL - CAP + k, sources, stride=TAIL), :]
    table = meta[...]
    coefs = table[:, :TERMS].astype(BF16)

    turned = table.T
    at = TERMS
    weight = turned[at + 8 : at + 9, :]
    row_start = turned[at + 9 : at + 10, :]
    row_taps = [
        (weight * turned[at + k : at + k + 1, :]).astype(BF16).astype(F32) for k in range(4)
    ]
    fields[...] = jnp.concatenate(row_taps + [turned[at + 4 : at + 8, :]], axis=0)
    whole[...] = jnp.concatenate(
        [turned[at + 9 : at + 11, :], jnp.zeros((6, slots), F32)], axis=0
    ).astype(jnp.int32)
    copies = [
        pltpu.make_async_copy(fields, fields_s, sem.at[0]),
        pltpu.make_async_copy(whole, whole_s, sem.at[1]),
    ]
    for copy in copies:
        copy.start()

    flat = iota((4 * BREADTH, 1), 0)
    seat = flat & (BREADTH - 1)
    turn = (seat * 3121) >> 16
    a = (flat >> 7) * SIDE + turn
    b = seat - turn * KERNEL
    outer = (b * 11) >> 5
    there = (b - INNER * outer) * PATCH + (outer >> 2) * BREADTH
    there = there + ((outer * HEIGHT + a - REACH) & (BREADTH - 1))
    there = jnp.where((turn < SIDE) & (a < KERNEL), there, -1)
    moved = jnp.where(iota((4 * BREADTH, INNER * PATCH), 1) == there, 1.0, 0.0).astype(BF16)
    arranged = dot(basis, moved).astype(BF16)
    made = dot(coefs, arranged).astype(BF16).astype(F32)
    for part in range(2 * INNER):
        kernels[part] = made[:, part * BREADTH : (part + 1) * BREADTH]

    gap = (iota((PATCH, slots), 0) + 1).astype(F32) - row_start
    row_weight = jnp.zeros((PATCH, slots), F32)
    for k in range(4):
        inside = (gap >= k) & (gap < HEIGHT + k)
        row_weight = row_weight + jnp.where(inside, row_taps[k], 0.0)
    gap = (iota((slots, PATCH), 1) + 1).astype(F32) - table[:, at + 10 : at + 11]
    col_weight = jnp.zeros((slots, PATCH), F32)
    for k in range(4):
        inside = (gap >= k) & (gap < BREADTH + k)
        col_weight = col_weight + jnp.where(inside, table[:, at + 4 + k : at + 5 + k], 0.0)
    row_high = row_weight.astype(BF16)
    row_low = (row_weight - row_high.astype(F32)).astype(BF16)
    col_high = col_weight.astype(BF16)
    col_low = (col_weight - col_high.astype(F32)).astype(BF16)
    depth = dot(row_high, col_high) + (dot(row_high, col_low) + dot(row_low, col_high))
    shares = PATCH // HEIGHT
    for v in range(shares):
        out[v, HEIGHT:, :] = depth[v * HEIGHT : (v + 1) * HEIGHT, :].astype(out.dtype)

    for copy in copies:
        copy.wait()

    numer[...] = jnp.zeros_like(numer)
    padded[...] = jnp.zeros_like(padded)
    lane = iota((HEIGHT, BREADTH), 1)
    line = iota((8, BREADTH), 1)
    apart = (lane & (HEIGHT - 1)) - iota((HEIGHT, BREADTH), 0)
    near_row = (apart <= REACH) & (apart >= -REACH)
    nothing = jnp.zeros((HEIGHT, BREADTH), BF16)
    per_cap = sources // GROUP

    def tall(x):
        return jnp.concatenate([x] * (WINDOW // 8), axis=0)

    def work(g, carry):
        k = g // per_cap
        first = (g - k * per_cap) * GROUP
        for q in range(GROUP):
            s = g * GROUP + q
            pixels = blocks[first + q, pl.ds(pl.multiple_of(k * HEIGHT, HEIGHT), HEIGHT), :]
            low, high = [], []
            for outer in range(OUTER):
                move = REACH - 1 - INNER * outer
                if move == 0:
                    low.append(pixels)
                    high.append(nothing)
                    continue
                moved = pltpu.roll(pixels.astype(F32), move % BREADTH, 1).astype(BF16)
                kept = lane >= move if move > 0 else lane < BREADTH + move
                low.append(jnp.where(kept, moved, nothing))
                high.append(jnp.where(kept, nothing, moved))
            low.append(nothing)
            high.append(nothing)
            shifted = jnp.concatenate(
                [jnp.concatenate(low, axis=0), jnp.concatenate(high, axis=0)], axis=1
            )
            halves = []
            for half in range(2):
                rows = []
                for inner in range(INNER):
                    row = kernels[2 * inner + half, pl.ds(s, 1), :]
                    turn = pltpu.roll(
                        jnp.broadcast_to(row, (HEIGHT, BREADTH)), 0, 1, stride=1, stride_axis=0
                    )
                    rows.append(jnp.where(near_row, turn, 0.0).astype(BF16))
                halves.append(jnp.concatenate(rows, axis=0))
            left = jnp.concatenate(halves, axis=1)
            product = dot(left, shifted)
            before, centre, after = (product[inner * HEIGHT : (inner + 1) * HEIGHT, :] for inner in range(INNER))
            before = jnp.where(lane == BREADTH - 1, before[:, BREADTH:], before[:, :BREADTH])
            after = jnp.where(lane == 0, after[:, BREADTH:], after[:, :BREADTH])
            total = centre[:, :BREADTH] + pltpu.roll(before, 1, 1) + pltpu.roll(after, BREADTH - 1, 1)
            row_at = whole_s[0, s]
            col_at = whole_s[1, s]
            padded[q, pl.ds(8, HEIGHT), :] = total.astype(BF16).astype(F32)
            tapped = fields_s[0, s] * padded[q, pl.ds(8, WINDOW), :]
            for t in range(1, 4):
                tapped = tapped + fields_s[t, s] * padded[q, pl.ds(8 - t, WINDOW), :]
            wide_low = wide_high = None
            for t in range(4):
                tap = fields_s[4 + t, s]
                start = col_at + (t - 1)
                near = jnp.where(line >= start, tap, 0.0)
                far = jnp.where(line < start, tap, 0.0)
                if t == 0:
                    near = jnp.where((line == BREADTH - 1) & (col_at == 0), 0.0, near)
                if t == 3:
                    far = jnp.where((line == 0) & (col_at == BREADTH - 1), 0.0, far)
                moved = pltpu.roll(tapped, lax.rem(start + BREADTH, BREADTH), 1)
                low_term, high_term = tall(near) * moved, tall(far) * moved
                wide_low = low_term if t == 0 else wide_low + low_term
                wide_high = high_term if t == 0 else wide_high + high_term
            numer[q % 2, 0, pl.ds(row_at + 7, WINDOW), :] += wide_low
            numer[q % 2, 1, pl.ds(row_at + 7, WINDOW), :] += wide_high
        return carry

    lax.fori_loop(0, groups, work, 0)
    for v in range(shares):
        rows = pl.ds(8 + v * HEIGHT, HEIGHT)
        for half in range(2):
            both = numer[0, half, rows, :] + numer[1, half, rows, :]
            out[v, :HEIGHT, half * BREADTH : (half + 1) * BREADTH] = both.astype(out.dtype)


def coadd_sums(blocks):
    sources = blocks.shape[0]
    slots = CAP * sources
    vmem = pl.BlockSpec(memory_space=pltpu.VMEM)
    return pl.pallas_call(
        functools.partial(coadd_body, sources),
        out_shape=jax.ShapeDtypeStruct((PATCH // HEIGHT, 2 * HEIGHT, PATCH), BF16),
        in_specs=[vmem],
        out_specs=vmem,
        scratch_shapes=[
            pltpu.VMEM((sources * TAIL, BREADTH), F32),
            pltpu.VMEM((slots, BREADTH), F32),
            pltpu.VMEM((2 * INNER, slots, BREADTH), F32),
            pltpu.VMEM((GROUP, 8 + HEIGHT + 8, BREADTH), F32),
            pltpu.VMEM((2, 2, PATCH + 16, BREADTH), F32),
            pltpu.VMEM((8, slots), F32),
            pltpu.VMEM((8, slots), jnp.int32),
            pltpu.SMEM((8, slots), F32),
            pltpu.SMEM((8, slots), jnp.int32),
            pltpu.SemaphoreType.DMA((2,)),
        ],
        compiler_params=pltpu.CompilerParams(vmem_limit_bytes=48 << 20),
        name="coadd",
    )(blocks)


def per_device(stamps, coefs, basis, taps, weights, target, row_offset, col_offset):
    places = lax.axis_size("patch")
    blocks = pack(
        target[:, :, 0], stamps[0], coefs[0].T, basis[0, 0], taps[0].T, weights, row_offset, col_offset, places
    )
    blocks = lax.all_to_all(blocks, "patch", split_axis=0, concat_axis=0, tiled=True)
    sums = coadd_sums(blocks)
    sums = lax.all_to_all(sums, "visit", split_axis=0, concat_axis=0, tiled=True)
    total = jnp.sum(sums.astype(F32), axis=0)
    depth_map = total[HEIGHT:]
    coadd = total[:HEIGHT] / (1.0 + depth_map)
    return (coadd[None], depth_map[None])


def solution(mesh):
    placed = (
        P("visit", "patch", None, None),
        P("visit", "patch", None),
        P("visit", "patch", None, None),
        P("visit", "patch", None),
        P("visit", "patch"),
        P("visit", "patch", None),
        P("visit", "patch"),
        P("visit", "patch"),
    )
    return jax.shard_map(
        per_device,
        mesh=mesh,
        in_specs=placed,
        out_specs=(P("patch", "visit", None), P("patch", "visit", None)),
        check_vma=False,
    )
```

```python
import functools

import jax
import jax.numpy as jnp
from jax import lax
from jax.experimental import pallas as pl
from jax.experimental.pallas import tpu as pltpu
from jax.sharding import PartitionSpec as P

BF16 = jnp.bfloat16
F32 = jnp.float32
KERNEL = 21
REACH = 10
TERMS = 64
HEIGHT = 32
BREADTH = 128
PATCH = 256
CAP = 4
TAIL = 8
BLOCK_ROWS = CAP * HEIGHT + TAIL
INNER = 3
OUTER = 7
WINDOW = HEIGHT + 8
GROUP = 8
OPERANDS = 9
SIDE = 6


def iota(shape, axis):
    return lax.broadcasted_iota(jnp.int32, shape, axis)


def dot(a, b):
    return jnp.dot(a, b, preferred_element_type=F32)


def pack_body(*refs):
    given, out, here, count, sem = refs[:OPERANDS], refs[OPERANDS], refs[OPERANDS + 1 : -2], refs[-2], refs[-1]
    target_s, target, coefs, basis, taps, weights, row_offset, col_offset, held = here
    places = out.shape[0]
    stamp_count = held.shape[0]
    fetches = [
        pltpu.make_async_copy(source, place, sem.at[n]) for n, (source, place) in enumerate(zip(given, here))
    ]
    for fetch in fetches:
        fetch.start()
    out[...] = jnp.zeros_like(out)
    for fetch in fetches[:-1]:
        fetch.wait()
    across = jnp.broadcast_to(target[...].astype(F32), (stamp_count, stamp_count))
    square = (stamp_count, stamp_count)
    earlier = (across.T == across) & (iota(square, 0) < iota(square, 1))
    rank = jnp.sum(jnp.where(earlier, 1.0, 0.0), axis=0, keepdims=True)
    place = target[...] * TAIL + (TAIL - CAP) + rank.astype(jnp.int32)
    chosen = jnp.where(iota((places * TAIL, stamp_count), 0) == place, 1.0, 0.0).astype(BF16)
    extras = jnp.concatenate(
        [
            coefs[...].astype(F32),
            taps[...].astype(F32),
            weights[...].astype(F32),
            row_offset[...].astype(F32),
            col_offset[...].astype(F32),
            jnp.zeros((BREADTH - TERMS - 11, stamp_count), F32),
        ],
        axis=0,
    )
    tail = lax.dot_general(
        chosen, extras.astype(BF16), (((1,), (1,)), ((), ())), preferred_element_type=F32
    )
    wide = jnp.pad(basis[...].astype(F32), ((0, 24 - KERNEL), (0, BREADTH - KERNEL)))
    seat = iota(wide.shape, 0)
    seat = seat - SIDE * ((seat * 11) >> 6)
    laid = jnp.where(seat == 0, wide, 0.0)
    for r in range(1, SIDE):
        laid = laid + jnp.where(seat == r, pltpu.roll(wide, r * KERNEL, 1), 0.0)
    fold = jnp.where((iota((TAIL, 24), 1) * 11) >> 6 == iota((TAIL, 24), 0), 1.0, 0.0)
    shared = dot(fold.astype(BF16), laid.astype(BF16))
    tail = tail.reshape(places, TAIL, BREADTH) + shared[None]
    out[:, CAP * HEIGHT :, :] = tail.astype(BF16)

    def clear(d, carry):
        count[d] = 0
        return carry

    lax.fori_loop(0, places, clear, 0, unroll=8)
    fetches[-1].wait()

    def put(s, carry):
        d = target_s[0, s]
        k = count[d]
        count[d] = k + 1
        out[d, pl.ds(pl.multiple_of(k * HEIGHT, HEIGHT), HEIGHT), :] = held[s]
        return carry

    lax.fori_loop(0, stamp_count, put, 0, unroll=4)


def pack(target, stamps, coefs, basis, taps, weights, row_offset, col_offset, places):
    given = (target, target, coefs, basis, taps, weights, row_offset, col_offset, stamps)
    here = [pltpu.SMEM(target.shape, jnp.int32)] + [pltpu.VMEM(x.shape, x.dtype) for x in given[1:]]
    return pl.pallas_call(
        pack_body,
        out_shape=jax.ShapeDtypeStruct((places, BLOCK_ROWS, BREADTH), BF16),
        in_specs=[pl.BlockSpec(memory_space=pltpu.HBM)] * OPERANDS,
        out_specs=pl.BlockSpec(memory_space=pltpu.VMEM),
        scratch_shapes=here + [pltpu.SMEM((places,), jnp.int32), pltpu.SemaphoreType.DMA((OPERANDS,))],
        compiler_params=pltpu.CompilerParams(vmem_limit_bytes=40 << 20),
        name="pack",
    )(*(pltpu.with_memory_space_constraint(x, pltpu.HBM) for x in given))


def coadd_body(
    sources, blocks, out, tail, meta, kernels, left_a, left_b, shifted_a, shifted_b, padded_a, padded_b,
    sum_a, sum_b, sum_c, sum_d, fields, whole, fields_s, whole_s, sem
):
    slots = CAP * sources
    groups = slots // GROUP
    tail[...] = blocks[:, CAP * HEIGHT :, :].astype(F32).reshape(sources * TAIL, BREADTH)
    basis = jnp.concatenate(
        [tail[pl.ds(q, sources, stride=TAIL), :] for q in range(TAIL - CAP)], axis=1
    ).astype(BF16)
    for k in range(CAP):
        meta[pl.ds(k * sources, sources), :] = tail[pl.ds(TAIL - CAP + k, sources, stride=TAIL), :]
    table = meta[...]
    coefs = table[:, :TERMS].astype(BF16)

    turned = table.T
    at = TERMS
    weight = turned[at + 8 : at + 9, :]
    row_start = turned[at + 9 : at + 10, :]
    row_taps = [
        (weight * turned[at + k : at + k + 1, :]).astype(BF16).astype(F32) for k in range(4)
    ]
    fields[...] = jnp.concatenate(row_taps + [turned[at + 4 : at + 8, :]], axis=0)
    whole[...] = jnp.concatenate(
        [turned[at + 9 : at + 11, :], jnp.zeros((6, slots), F32)], axis=0
    ).astype(jnp.int32)
    copies = [
        pltpu.make_async_copy(fields, fields_s, sem.at[0]),
        pltpu.make_async_copy(whole, whole_s, sem.at[1]),
    ]
    for copy in copies:
        copy.start()

    flat = iota((4 * BREADTH, 1), 0)
    seat = flat & (BREADTH - 1)
    turn = (seat * 3121) >> 16
    a = (flat >> 7) * SIDE + turn
    b = seat - turn * KERNEL
    outer = (b * 11) >> 5
    there = (b - INNER * outer) * PATCH + (outer >> 2) * BREADTH
    there = there + ((outer * HEIGHT + a - REACH) & (BREADTH - 1))
    there = jnp.where((turn < SIDE) & (a < KERNEL), there, -1)
    moved = jnp.where(iota((4 * BREADTH, INNER * PATCH), 1) == there, 1.0, 0.0).astype(BF16)
    arranged = dot(basis, moved).astype(BF16)
    made = dot(coefs, arranged).astype(BF16).astype(F32)
    for part in range(2 * INNER):
        kernels[part] = made[:, part * BREADTH : (part + 1) * BREADTH]

    gap = (iota((PATCH, slots), 0) + 1).astype(F32) - row_start
    row_weight = jnp.zeros((PATCH, slots), F32)
    for k in range(4):
        inside = (gap >= k) & (gap < HEIGHT + k)
        row_weight = row_weight + jnp.where(inside, row_taps[k], 0.0)
    gap = (iota((slots, PATCH), 1) + 1).astype(F32) - table[:, at + 10 : at + 11]
    col_weight = jnp.zeros((slots, PATCH), F32)
    for k in range(4):
        inside = (gap >= k) & (gap < BREADTH + k)
        col_weight = col_weight + jnp.where(inside, table[:, at + 4 + k : at + 5 + k], 0.0)
    row_high = row_weight.astype(BF16)
    row_low = (row_weight - row_high.astype(F32)).astype(BF16)
    col_high = col_weight.astype(BF16)
    col_low = (col_weight - col_high.astype(F32)).astype(BF16)
    depth = dot(row_high, col_high) + (dot(row_high, col_low) + dot(row_low, col_high))
    shares = PATCH // HEIGHT
    for v in range(shares):
        out[v, HEIGHT:, :] = depth[v * HEIGHT : (v + 1) * HEIGHT, :].astype(out.dtype)

    for copy in copies:
        copy.wait()

    sums = (sum_a, sum_b, sum_c, sum_d)
    for ref in sums + (padded_a, padded_b):
        ref[...] = jnp.zeros_like(ref)
    lane = iota((HEIGHT, BREADTH), 1)
    line = iota((8, BREADTH), 1)
    apart = (lane & (HEIGHT - 1)) - iota((HEIGHT, BREADTH), 0)
    near_row = (apart <= REACH) & (apart >= -REACH)
    nothing = jnp.zeros((HEIGHT, BREADTH), BF16)
    per_cap = sources // GROUP

    def tall(x):
        return jnp.concatenate([x] * (WINDOW // 8), axis=0)

    def build(g, left, shifted):
        k = g // per_cap
        first = (g - k * per_cap) * GROUP
        for q in range(GROUP):
            pixels = blocks[first + q, pl.ds(pl.multiple_of(k * HEIGHT, HEIGHT), HEIGHT), :]
            for outer in range(OUTER):
                at = pl.ds(outer * HEIGHT, HEIGHT)
                move = REACH - 1 - INNER * outer
                if move == 0:
                    shifted[q, at, :BREADTH] = pixels
                    continue
                moved = pltpu.roll(pixels.astype(F32), move % BREADTH, 1).astype(BF16)
                kept = lane >= move if move > 0 else lane < BREADTH + move
                shifted[q, at, :BREADTH] = jnp.where(kept, moved, nothing)
                shifted[q, at, BREADTH:] = jnp.where(kept, nothing, moved)
            for inner in range(INNER):
                for half in range(2):
                    row = kernels[2 * inner + half, pl.ds(g * GROUP + q, 1), :]
                    turn = pltpu.roll(
                        jnp.broadcast_to(row, (HEIGHT, BREADTH)), 0, 1, stride=1, stride_axis=0
                    )
                    left[q, pl.ds(inner * HEIGHT, HEIGHT), half * BREADTH : (half + 1) * BREADTH] = jnp.where(
                        near_row, turn, 0.0
                    ).astype(BF16)

    def convolve(left, shifted, padded):
        for q in range(GROUP):
            product = dot(left[q], shifted[q])
            before, centre, after = (product[inner * HEIGHT : (inner + 1) * HEIGHT, :] for inner in range(INNER))
            before = jnp.where(lane == BREADTH - 1, before[:, BREADTH:], before[:, :BREADTH])
            after = jnp.where(lane == 0, after[:, BREADTH:], after[:, :BREADTH])
            total = centre[:, :BREADTH] + pltpu.roll(before, 1, 1) + pltpu.roll(after, BREADTH - 1, 1)
            padded[q, pl.ds(8, HEIGHT), :] = total.astype(BF16).astype(F32)

    def resample(g, padded):
        for q in range(GROUP):
            s = g * GROUP + q
            row_at = whole_s[0, s]
            col_at = whole_s[1, s]
            tapped = fields_s[0, s] * padded[q, pl.ds(8, WINDOW), :]
            for t in range(1, 4):
                tapped = tapped + fields_s[t, s] * padded[q, pl.ds(8 - t, WINDOW), :]
            wide_low = wide_high = None
            for t in range(4):
                tap = fields_s[4 + t, s]
                start = col_at + (t - 1)
                near = jnp.where(line >= start, tap, 0.0)
                far = jnp.where(line < start, tap, 0.0)
                if t == 0:
                    near = jnp.where((line == BREADTH - 1) & (col_at == 0), 0.0, near)
                if t == 3:
                    far = jnp.where((line == 0) & (col_at == BREADTH - 1), 0.0, far)
                moved = pltpu.roll(tapped, lax.rem(start + BREADTH, BREADTH), 1)
                low_term, high_term = tall(near) * moved, tall(far) * moved
                wide_low = low_term if t == 0 else wide_low + low_term
                wide_high = high_term if t == 0 else wide_high + high_term
            low, high = sums[2 * (q % 2)], sums[2 * (q % 2) + 1]
            low[pl.ds(row_at + 7, WINDOW), :] += wide_low
            high[pl.ds(row_at + 7, WINDOW), :] += wide_high

    for ref in (shifted_a, shifted_b):
        ref[...] = jnp.zeros_like(ref)
    build(0, left_a, shifted_a)

    def work(h, carry):
        g = 2 * h
        build(g + 1, left_b, shifted_b)
        convolve(left_a, shifted_a, padded_a)
        resample(jnp.maximum(g - 1, 0), padded_b)
        build(jnp.minimum(g + 2, groups - 1), left_a, shifted_a)
        convolve(left_b, shifted_b, padded_b)
        resample(g, padded_a)
        return carry

    lax.fori_loop(0, groups // 2, work, 0)
    resample(groups - 1, padded_b)
    for v in range(shares):
        rows = pl.ds(8 + v * HEIGHT, HEIGHT)
        for half in range(2):
            both = sums[half][rows, :] + sums[2 + half][rows, :]
            out[v, :HEIGHT, half * BREADTH : (half + 1) * BREADTH] = both.astype(out.dtype)


def coadd_sums(blocks):
    sources = blocks.shape[0]
    slots = CAP * sources
    vmem = pl.BlockSpec(memory_space=pltpu.VMEM)
    return pl.pallas_call(
        functools.partial(coadd_body, sources),
        out_shape=jax.ShapeDtypeStruct((PATCH // HEIGHT, 2 * HEIGHT, PATCH), BF16),
        in_specs=[vmem],
        out_specs=vmem,
        scratch_shapes=[
            pltpu.VMEM((sources * TAIL, BREADTH), F32),
            pltpu.VMEM((slots, BREADTH), F32),
            pltpu.VMEM((2 * INNER, slots, BREADTH), F32),
            pltpu.VMEM((GROUP, INNER * HEIGHT, PATCH), BF16),
            pltpu.VMEM((GROUP, INNER * HEIGHT, PATCH), BF16),
            pltpu.VMEM((GROUP, PATCH, PATCH), BF16),
            pltpu.VMEM((GROUP, PATCH, PATCH), BF16),
            pltpu.VMEM((GROUP, 8 + HEIGHT + 8, BREADTH), F32),
            pltpu.VMEM((GROUP, 8 + HEIGHT + 8, BREADTH), F32),
            pltpu.VMEM((PATCH + 16, BREADTH), F32),
            pltpu.VMEM((PATCH + 16, BREADTH), F32),
            pltpu.VMEM((PATCH + 16, BREADTH), F32),
            pltpu.VMEM((PATCH + 16, BREADTH), F32),
            pltpu.VMEM((8, slots), F32),
            pltpu.VMEM((8, slots), jnp.int32),
            pltpu.SMEM((8, slots), F32),
            pltpu.SMEM((8, slots), jnp.int32),
            pltpu.SemaphoreType.DMA((2,)),
        ],
        compiler_params=pltpu.CompilerParams(vmem_limit_bytes=48 << 20),
        name="coadd",
    )(blocks)


def per_device(stamps, coefs, basis, taps, weights, target, row_offset, col_offset):
    places = lax.axis_size("patch")
    blocks = pack(
        target[:, :, 0], stamps[0], coefs[0].T, basis[0, 0], taps[0].T, weights, row_offset, col_offset, places
    )
    blocks = lax.all_to_all(blocks, "patch", split_axis=0, concat_axis=0, tiled=True)
    sums = coadd_sums(blocks)
    sums = lax.all_to_all(sums, "visit", split_axis=0, concat_axis=0, tiled=True)
    total = jnp.sum(sums.astype(F32), axis=0)
    depth_map = total[HEIGHT:]
    coadd = total[:HEIGHT] / (1.0 + depth_map)
    return (coadd[None], depth_map[None])


def solution(mesh):
    placed = (
        P("visit", "patch", None, None),
        P("visit", "patch", None),
        P("visit", "patch", None, None),
        P("visit", "patch", None),
        P("visit", "patch"),
        P("visit", "patch", None),
        P("visit", "patch"),
        P("visit", "patch"),
    )
    return jax.shard_map(
        per_device,
        mesh=mesh,
        in_specs=placed,
        out_specs=(P("patch", "visit", None), P("patch", "visit", None)),
        check_vma=False,
    )
```

```python
import functools

import jax
import jax.numpy as jnp
from jax import lax
from jax.experimental import pallas as pl
from jax.experimental.pallas import tpu as pltpu
from jax.sharding import PartitionSpec as P

BF16 = jnp.bfloat16
F32 = jnp.float32
KERNEL = 21
REACH = 10
TERMS = 64
HEIGHT = 32
BREADTH = 128
PATCH = 256
CAP = 4
EARLY = 3
TAIL = 8
BLOCK_ROWS = EARLY * HEIGHT + TAIL
INNER = 3
OUTER = 7
WINDOW = HEIGHT + 8
GROUP = 8
OPERANDS = 9
SIDE = 6


def iota(shape, axis):
    return lax.broadcasted_iota(jnp.int32, shape, axis)


def dot(a, b):
    return jnp.dot(a, b, preferred_element_type=F32)


def pack_body(*refs):
    given, (out, late), here = refs[:OPERANDS], refs[OPERANDS : OPERANDS + 2], refs[OPERANDS + 2 : -2]
    count, sem = refs[-2], refs[-1]
    target_s, target, coefs, basis, taps, weights, row_offset, col_offset, held = here
    places = out.shape[0]
    stamp_count = held.shape[0]
    fetches = [
        pltpu.make_async_copy(source, place, sem.at[n]) for n, (source, place) in enumerate(zip(given, here))
    ]
    for fetch in fetches:
        fetch.start()
    out[...] = jnp.zeros_like(out)
    late[...] = jnp.zeros_like(late)
    for fetch in fetches[:-1]:
        fetch.wait()
    across = jnp.broadcast_to(target[...].astype(F32), (stamp_count, stamp_count))
    square = (stamp_count, stamp_count)
    earlier = (across.T == across) & (iota(square, 0) < iota(square, 1))
    rank = jnp.sum(jnp.where(earlier, 1.0, 0.0), axis=0, keepdims=True)
    place = target[...] * TAIL + (TAIL - CAP) + rank.astype(jnp.int32)
    chosen = jnp.where(iota((places * TAIL, stamp_count), 0) == place, 1.0, 0.0).astype(BF16)
    extras = jnp.concatenate(
        [
            coefs[...].astype(F32),
            taps[...].astype(F32),
            weights[...].astype(F32),
            row_offset[...].astype(F32),
            col_offset[...].astype(F32),
            jnp.zeros((BREADTH - TERMS - 11, stamp_count), F32),
        ],
        axis=0,
    )
    tail = lax.dot_general(
        chosen, extras.astype(BF16), (((1,), (1,)), ((), ())), preferred_element_type=F32
    )
    wide = jnp.pad(basis[...].astype(F32), ((0, 24 - KERNEL), (0, BREADTH - KERNEL)))
    seat = iota(wide.shape, 0)
    seat = seat - SIDE * ((seat * 11) >> 6)
    laid = jnp.where(seat == 0, wide, 0.0)
    for r in range(1, SIDE):
        laid = laid + jnp.where(seat == r, pltpu.roll(wide, r * KERNEL, 1), 0.0)
    fold = jnp.where((iota((TAIL, 24), 1) * 11) >> 6 == iota((TAIL, 24), 0), 1.0, 0.0)
    shared = dot(fold.astype(BF16), laid.astype(BF16))
    tail = tail.reshape(places, TAIL, BREADTH) + shared[None]
    out[:, EARLY * HEIGHT :, :] = tail.astype(BF16)

    def clear(d, carry):
        count[d] = 0
        return carry

    lax.fori_loop(0, places, clear, 0, unroll=8)
    fetches[-1].wait()

    def put(s, carry):
        d = target_s[0, s]
        k = count[d]
        count[d] = k + 1
        stamp = held[s]
        at = pl.ds(pl.multiple_of(jnp.minimum(k, EARLY - 1) * HEIGHT, HEIGHT), HEIGHT)
        out[d, at, :] = jnp.where(k < EARLY, stamp, out[d, at, :])
        late[d] = stamp
        return carry

    lax.fori_loop(0, stamp_count, put, 0, unroll=4)


def pack(target, stamps, coefs, basis, taps, weights, row_offset, col_offset, places):
    given = (target, target, coefs, basis, taps, weights, row_offset, col_offset, stamps)
    here = [pltpu.SMEM(target.shape, jnp.int32)] + [pltpu.VMEM(x.shape, x.dtype) for x in given[1:]]
    return pl.pallas_call(
        pack_body,
        out_shape=[jax.ShapeDtypeStruct((places, rows, BREADTH), BF16) for rows in (BLOCK_ROWS, HEIGHT)],
        in_specs=[pl.BlockSpec(memory_space=pltpu.HBM)] * OPERANDS,
        out_specs=[pl.BlockSpec(memory_space=pltpu.VMEM)] * 2,
        scratch_shapes=here + [pltpu.SMEM((places,), jnp.int32), pltpu.SemaphoreType.DMA((OPERANDS,))],
        compiler_params=pltpu.CompilerParams(vmem_limit_bytes=40 << 20),
        name="pack",
    )(*(pltpu.with_memory_space_constraint(x, pltpu.HBM) for x in given))


def add_slots(blocks, kernels, fields_s, whole_s, base, groups, sums, buffers):
    left_a, left_b, shifted_a, shifted_b, padded_a, padded_b = buffers
    lane = iota((HEIGHT, BREADTH), 1)
    line = iota((8, BREADTH), 1)
    apart = (lane & (HEIGHT - 1)) - iota((HEIGHT, BREADTH), 0)
    near_row = (apart <= REACH) & (apart >= -REACH)
    nothing = jnp.zeros((HEIGHT, BREADTH), BF16)
    per_cap = blocks.shape[0] // GROUP

    def tall(x):
        return jnp.concatenate([x] * (WINDOW // 8), axis=0)

    def build(g, left, shifted):
        k = g // per_cap
        first = (g - k * per_cap) * GROUP
        for q in range(GROUP):
            pixels = blocks[first + q, pl.ds(pl.multiple_of(k * HEIGHT, HEIGHT), HEIGHT), :]
            for outer in range(OUTER):
                at = pl.ds(outer * HEIGHT, HEIGHT)
                move = REACH - 1 - INNER * outer
                if move == 0:
                    shifted[q, at, :BREADTH] = pixels
                    continue
                moved = pltpu.roll(pixels.astype(F32), move % BREADTH, 1).astype(BF16)
                kept = lane >= move if move > 0 else lane < BREADTH + move
                shifted[q, at, :BREADTH] = jnp.where(kept, moved, nothing)
                shifted[q, at, BREADTH:] = jnp.where(kept, nothing, moved)
            for inner in range(INNER):
                for half in range(2):
                    row = kernels[2 * inner + half, pl.ds(g * GROUP + q, 1), :]
                    turn = pltpu.roll(
                        jnp.broadcast_to(row, (HEIGHT, BREADTH)), 0, 1, stride=1, stride_axis=0
                    )
                    left[q, pl.ds(inner * HEIGHT, HEIGHT), half * BREADTH : (half + 1) * BREADTH] = jnp.where(
                        near_row, turn, 0.0
                    ).astype(BF16)

    def convolve(left, shifted, padded):
        for q in range(GROUP):
            product = dot(left[q], shifted[q])
            before, centre, after = (product[inner * HEIGHT : (inner + 1) * HEIGHT, :] for inner in range(INNER))
            before = jnp.where(lane == BREADTH - 1, before[:, BREADTH:], before[:, :BREADTH])
            after = jnp.where(lane == 0, after[:, BREADTH:], after[:, :BREADTH])
            total = centre[:, :BREADTH] + pltpu.roll(before, 1, 1) + pltpu.roll(after, BREADTH - 1, 1)
            padded[q, pl.ds(8, HEIGHT), :] = total.astype(BF16).astype(F32)

    def resample(g, padded):
        for q in range(GROUP):
            s = base + g * GROUP + q
            row_at = whole_s[0, s]
            col_at = whole_s[1, s]
            tapped = fields_s[0, s] * padded[q, pl.ds(8, WINDOW), :]
            for t in range(1, 4):
                tapped = tapped + fields_s[t, s] * padded[q, pl.ds(8 - t, WINDOW), :]
            wide_low = wide_high = None
            for t in range(4):
                tap = fields_s[4 + t, s]
                start = col_at + (t - 1)
                near = jnp.where(line >= start, tap, 0.0)
                far = jnp.where(line < start, tap, 0.0)
                if t == 0:
                    near = jnp.where((line == BREADTH - 1) & (col_at == 0), 0.0, near)
                if t == 3:
                    far = jnp.where((line == 0) & (col_at == BREADTH - 1), 0.0, far)
                moved = pltpu.roll(tapped, lax.rem(start + BREADTH, BREADTH), 1)
                low_term, high_term = tall(near) * moved, tall(far) * moved
                wide_low = low_term if t == 0 else wide_low + low_term
                wide_high = high_term if t == 0 else wide_high + high_term
            low, high = sums.at[2 * (q % 2)], sums.at[2 * (q % 2) + 1]
            low[pl.ds(row_at + 7, WINDOW), :] += wide_low
            high[pl.ds(row_at + 7, WINDOW), :] += wide_high

    for ref in (shifted_a, shifted_b, padded_a, padded_b):
        ref[...] = jnp.zeros_like(ref)
    build(0, left_a, shifted_a)

    def work(h, carry):
        g = 2 * h
        build(g + 1, left_b, shifted_b)
        convolve(left_a, shifted_a, padded_a)
        resample(jnp.maximum(g - 1, 0), padded_b)
        build(jnp.minimum(g + 2, groups - 1), left_a, shifted_a)
        convolve(left_b, shifted_b, padded_b)
        resample(g, padded_a)
        return carry

    lax.fori_loop(0, groups // 2, work, 0)
    resample(groups - 1, padded_b)


def first_body(blocks, sums, late_kernels, fields, whole, depths, tail, meta, kernels, fields_s, whole_s, sem, *buffers):
    sources = blocks.shape[0]
    slots = CAP * sources
    tail[...] = blocks[:, EARLY * HEIGHT :, :].astype(F32).reshape(sources * TAIL, BREADTH)
    basis = jnp.concatenate(
        [tail[pl.ds(q, sources, stride=TAIL), :] for q in range(TAIL - CAP)], axis=1
    ).astype(BF16)
    for k in range(CAP):
        meta[pl.ds(k * sources, sources), :] = tail[pl.ds(TAIL - CAP + k, sources, stride=TAIL), :]
    table = meta[...]
    coefs = table[:, :TERMS].astype(BF16)

    turned = table.T
    at = TERMS
    weight = turned[at + 8 : at + 9, :]
    row_start = turned[at + 9 : at + 10, :]
    row_taps = [
        (weight * turned[at + k : at + k + 1, :]).astype(BF16).astype(F32) for k in range(4)
    ]
    fields[...] = jnp.concatenate(row_taps + [turned[at + 4 : at + 8, :]], axis=0)
    whole[...] = jnp.concatenate(
        [turned[at + 9 : at + 11, :], jnp.zeros((6, slots), F32)], axis=0
    ).astype(jnp.int32)
    copies = [
        pltpu.make_async_copy(fields, fields_s, sem.at[0]),
        pltpu.make_async_copy(whole, whole_s, sem.at[1]),
    ]
    for copy in copies:
        copy.start()

    flat = iota((4 * BREADTH, 1), 0)
    seat = flat & (BREADTH - 1)
    turn = (seat * 3121) >> 16
    a = (flat >> 7) * SIDE + turn
    b = seat - turn * KERNEL
    outer = (b * 11) >> 5
    there = (b - INNER * outer) * PATCH + (outer >> 2) * BREADTH
    there = there + ((outer * HEIGHT + a - REACH) & (BREADTH - 1))
    there = jnp.where((turn < SIDE) & (a < KERNEL), there, -1)
    moved = jnp.where(iota((4 * BREADTH, INNER * PATCH), 1) == there, 1.0, 0.0).astype(BF16)
    arranged = dot(basis, moved).astype(BF16)
    made = dot(coefs, arranged).astype(BF16).astype(F32)
    early = EARLY * sources
    for part in range(2 * INNER):
        at_part = slice(part * BREADTH, (part + 1) * BREADTH)
        kernels[part] = made[:early, at_part]
        late_kernels[part] = made[early:, at_part]

    gap = (iota((PATCH, slots), 0) + 1).astype(F32) - row_start
    row_weight = jnp.zeros((PATCH, slots), F32)
    for k in range(4):
        inside = (gap >= k) & (gap < HEIGHT + k)
        row_weight = row_weight + jnp.where(inside, row_taps[k], 0.0)
    gap = (iota((slots, PATCH), 1) + 1).astype(F32) - table[:, at + 10 : at + 11]
    col_weight = jnp.zeros((slots, PATCH), F32)
    for k in range(4):
        inside = (gap >= k) & (gap < BREADTH + k)
        col_weight = col_weight + jnp.where(inside, table[:, at + 4 + k : at + 5 + k], 0.0)
    row_high = row_weight.astype(BF16)
    row_low = (row_weight - row_high.astype(F32)).astype(BF16)
    col_high = col_weight.astype(BF16)
    col_low = (col_weight - col_high.astype(F32)).astype(BF16)
    depth = dot(row_high, col_high) + (dot(row_high, col_low) + dot(row_low, col_high))
    shares = PATCH // HEIGHT
    for v in range(shares):
        depths[v] = depth[v * HEIGHT : (v + 1) * HEIGHT, :].astype(depths.dtype)

    sums[...] = jnp.zeros_like(sums)
    for copy in copies:
        copy.wait()
    add_slots(blocks, kernels, fields_s, whole_s, 0, EARLY * sources // GROUP, sums, buffers)


def last_body(blocks, before, kernels, fields_s, whole_s, depths, out, sums, *buffers):
    sources = blocks.shape[0]
    sums[...] = before[...]
    add_slots(
        blocks, kernels, fields_s, whole_s, EARLY * sources, (CAP - EARLY) * sources // GROUP, sums, buffers
    )
    for v in range(PATCH // HEIGHT):
        rows = pl.ds(8 + v * HEIGHT, HEIGHT)
        for half in range(2):
            both = sums[half, rows, :] + sums[2 + half, rows, :]
            out[v, :HEIGHT, half * BREADTH : (half + 1) * BREADTH] = both.astype(out.dtype)
        out[v, HEIGHT:, :] = depths[v]


def buffer_shapes():
    return (
        [pltpu.VMEM((GROUP, INNER * HEIGHT, PATCH), BF16)] * 2
        + [pltpu.VMEM((GROUP, PATCH, PATCH), BF16)] * 2
        + [pltpu.VMEM((GROUP, 8 + HEIGHT + 8, BREADTH), F32)] * 2
    )


def sum_shape():
    return (4, PATCH + 16, BREADTH)


def cost(slots):
    return pl.CostEstimate(flops=slots * 80_000_000, bytes_accessed=slots * 8192, transcendentals=0)


def coadd_first(blocks):
    sources = blocks.shape[0]
    slots = CAP * sources
    vmem = pl.BlockSpec(memory_space=pltpu.VMEM)
    return pl.pallas_call(
        first_body,
        out_shape=[
            jax.ShapeDtypeStruct(sum_shape(), F32),
            jax.ShapeDtypeStruct((2 * INNER, slots - EARLY * sources, BREADTH), F32),
            jax.ShapeDtypeStruct((8, slots), F32),
            jax.ShapeDtypeStruct((8, slots), jnp.int32),
            jax.ShapeDtypeStruct((PATCH // HEIGHT, HEIGHT, PATCH), BF16),
        ],
        in_specs=[vmem],
        out_specs=[vmem] * 5,
        scratch_shapes=[
            pltpu.VMEM((sources * TAIL, BREADTH), F32),
            pltpu.VMEM((slots, BREADTH), F32),
            pltpu.VMEM((2 * INNER, EARLY * sources, BREADTH), F32),
            pltpu.SMEM((8, slots), F32),
            pltpu.SMEM((8, slots), jnp.int32),
            pltpu.SemaphoreType.DMA((2,)),
        ]
        + buffer_shapes(),
        compiler_params=pltpu.CompilerParams(vmem_limit_bytes=40 << 20),
        cost_estimate=cost(EARLY * sources),
        name="coadd_first",
    )(blocks)


def coadd_last(blocks, before, kernels, fields, whole, depths):
    vmem = pl.BlockSpec(memory_space=pltpu.VMEM)
    smem = pl.BlockSpec(memory_space=pltpu.SMEM)
    return pl.pallas_call(
        last_body,
        out_shape=jax.ShapeDtypeStruct((PATCH // HEIGHT, 2 * HEIGHT, PATCH), BF16),
        in_specs=[vmem, vmem, vmem, smem, smem, vmem],
        out_specs=vmem,
        scratch_shapes=[pltpu.VMEM(sum_shape(), F32)] + buffer_shapes(),
        compiler_params=pltpu.CompilerParams(vmem_limit_bytes=40 << 20),
        cost_estimate=cost((CAP - EARLY) * blocks.shape[0]),
        name="coadd_last",
    )(blocks, before, kernels, fields, whole, depths)


def per_device(stamps, coefs, basis, taps, weights, target, row_offset, col_offset):
    places = lax.axis_size("patch")
    early, late = pack(
        target[:, :, 0], stamps[0], coefs[0].T, basis[0, 0], taps[0].T, weights, row_offset, col_offset, places
    )
    early = lax.all_to_all(early, "patch", split_axis=0, concat_axis=0, tiled=True)
    early, late = lax.optimization_barrier((early, late))
    late = lax.all_to_all(late, "patch", split_axis=0, concat_axis=0, tiled=True)
    sums = coadd_last(late, *coadd_first(early))
    sums = lax.all_to_all(sums, "visit", split_axis=0, concat_axis=0, tiled=True)
    total = jnp.sum(sums.astype(F32), axis=0)
    depth_map = total[HEIGHT:]
    coadd = total[:HEIGHT] / (1.0 + depth_map)
    return (coadd[None], depth_map[None])


def solution(mesh):
    placed = (
        P("visit", "patch", None, None),
        P("visit", "patch", None),
        P("visit", "patch", None, None),
        P("visit", "patch", None),
        P("visit", "patch"),
        P("visit", "patch", None),
        P("visit", "patch"),
        P("visit", "patch"),
    )
    return jax.shard_map(
        per_device,
        mesh=mesh,
        in_specs=placed,
        out_specs=(P("patch", "visit", None), P("patch", "visit", None)),
        check_vma=False,
    )
```

```python
import functools

import jax
import jax.numpy as jnp
from jax import lax
from jax.experimental import pallas as pl
from jax.experimental.pallas import tpu as pltpu
from jax.sharding import PartitionSpec as P

BF16 = jnp.bfloat16
F32 = jnp.float32
KERNEL = 21
REACH = 10
TERMS = 64
HEIGHT = 32
BREADTH = 128
PATCH = 256
CAP = 4
TAIL = 8
BLOCK_ROWS = CAP * HEIGHT + TAIL
INNER = 3
OUTER = 7
WINDOW = HEIGHT + 8
GROUP = 8
OPERANDS = 9
SIDE = 6


def iota(shape, axis):
    return lax.broadcasted_iota(jnp.int32, shape, axis)


def dot(a, b):
    return jnp.dot(a, b, preferred_element_type=F32)


def pack_body(*refs):
    given, out, here, count, sem = refs[:OPERANDS], refs[OPERANDS], refs[OPERANDS + 1 : -2], refs[-2], refs[-1]
    target_s, target, coefs, basis, taps, weights, row_offset, col_offset, held = here
    places = out.shape[0]
    stamp_count = held.shape[0]
    fetches = [
        pltpu.make_async_copy(source, place, sem.at[n]) for n, (source, place) in enumerate(zip(given, here))
    ]
    for fetch in fetches:
        fetch.start()
    out[...] = jnp.zeros_like(out)
    for fetch in fetches[:-1]:
        fetch.wait()
    across = jnp.broadcast_to(target[...].astype(F32), (stamp_count, stamp_count))
    square = (stamp_count, stamp_count)
    earlier = (across.T == across) & (iota(square, 0) < iota(square, 1))
    rank = jnp.sum(jnp.where(earlier, 1.0, 0.0), axis=0, keepdims=True)
    place = target[...] * TAIL + (TAIL - CAP) + rank.astype(jnp.int32)
    chosen = jnp.where(iota((places * TAIL, stamp_count), 0) == place, 1.0, 0.0).astype(BF16)
    extras = jnp.concatenate(
        [
            coefs[...].astype(F32),
            taps[...].astype(F32),
            weights[...].astype(F32),
            row_offset[...].astype(F32),
            col_offset[...].astype(F32),
            jnp.zeros((BREADTH - TERMS - 11, stamp_count), F32),
        ],
        axis=0,
    )
    tail = lax.dot_general(
        chosen, extras.astype(BF16), (((1,), (1,)), ((), ())), preferred_element_type=F32
    )
    wide = jnp.pad(basis[...].astype(F32), ((0, 24 - KERNEL), (0, BREADTH - KERNEL)))
    seat = iota(wide.shape, 0)
    seat = seat - SIDE * ((seat * 11) >> 6)
    laid = jnp.where(seat == 0, wide, 0.0)
    for r in range(1, SIDE):
        laid = laid + jnp.where(seat == r, pltpu.roll(wide, r * KERNEL, 1), 0.0)
    fold = jnp.where((iota((TAIL, 24), 1) * 11) >> 6 == iota((TAIL, 24), 0), 1.0, 0.0)
    shared = dot(fold.astype(BF16), laid.astype(BF16))
    tail = tail.reshape(places, TAIL, BREADTH) + shared[None]
    out[:, CAP * HEIGHT :, :] = tail.astype(BF16)

    def clear(d, carry):
        count[d] = 0
        return carry

    lax.fori_loop(0, places, clear, 0, unroll=8)
    fetches[-1].wait()

    def put(s, carry):
        d = target_s[0, s]
        k = count[d]
        count[d] = k + 1
        out[d, pl.ds(pl.multiple_of(k * HEIGHT, HEIGHT), HEIGHT), :] = held[s]
        return carry

    lax.fori_loop(0, stamp_count, put, 0, unroll=4)


def pack(target, stamps, coefs, basis, taps, weights, row_offset, col_offset, places):
    given = (target, target, coefs, basis, taps, weights, row_offset, col_offset, stamps)
    here = [pltpu.SMEM(target.shape, jnp.int32)] + [pltpu.VMEM(x.shape, x.dtype) for x in given[1:]]
    return pl.pallas_call(
        pack_body,
        out_shape=jax.ShapeDtypeStruct((places, BLOCK_ROWS, BREADTH), BF16),
        in_specs=[pl.BlockSpec(memory_space=pltpu.HBM)] * OPERANDS,
        out_specs=pl.BlockSpec(memory_space=pltpu.VMEM),
        scratch_shapes=here + [pltpu.SMEM((places,), jnp.int32), pltpu.SemaphoreType.DMA((OPERANDS,))],
        compiler_params=pltpu.CompilerParams(vmem_limit_bytes=40 << 20),
        name="pack",
    )(*(pltpu.with_memory_space_constraint(x, pltpu.HBM) for x in given))


def coadd_body(
    sources, blocks, out, tail, meta, kernels, left_a, left_b, shifted_a, shifted_b, padded_a, padded_b,
    sum_a, sum_b, sum_c, sum_d, fields, whole, fields_s, whole_s, sem
):
    slots = CAP * sources
    groups = slots // GROUP
    tail[...] = blocks[:, CAP * HEIGHT :, :].astype(F32).reshape(sources * TAIL, BREADTH)
    basis = jnp.concatenate(
        [tail[pl.ds(q, sources, stride=TAIL), :] for q in range(TAIL - CAP)], axis=1
    ).astype(BF16)
    for k in range(CAP):
        meta[pl.ds(k * sources, sources), :] = tail[pl.ds(TAIL - CAP + k, sources, stride=TAIL), :]
    table = meta[...]
    coefs = table[:, :TERMS].astype(BF16)

    turned = table.T
    at = TERMS
    weight = turned[at + 8 : at + 9, :]
    row_start = turned[at + 9 : at + 10, :]
    row_taps = [
        (weight * turned[at + k : at + k + 1, :]).astype(BF16).astype(F32) for k in range(4)
    ]
    fields[...] = jnp.concatenate(row_taps + [turned[at + 4 : at + 8, :]], axis=0)
    whole[...] = jnp.concatenate(
        [turned[at + 9 : at + 11, :], jnp.zeros((6, slots), F32)], axis=0
    ).astype(jnp.int32)
    copies = [
        pltpu.make_async_copy(fields, fields_s, sem.at[0]),
        pltpu.make_async_copy(whole, whole_s, sem.at[1]),
    ]
    for copy in copies:
        copy.start()

    flat = iota((4 * BREADTH, 1), 0)
    seat = flat & (BREADTH - 1)
    turn = (seat * 3121) >> 16
    a = (flat >> 7) * SIDE + turn
    b = seat - turn * KERNEL
    outer = (b * 11) >> 5
    there = (b - INNER * outer) * PATCH + (outer >> 2) * BREADTH
    there = there + ((outer * HEIGHT + a - REACH) & (BREADTH - 1))
    there = jnp.where((turn < SIDE) & (a < KERNEL), there, -1)
    moved = jnp.where(iota((4 * BREADTH, INNER * PATCH), 1) == there, 1.0, 0.0).astype(BF16)
    arranged = dot(basis, moved).astype(BF16)
    made = dot(coefs, arranged).astype(BF16).astype(F32)
    for part in range(2 * INNER):
        kernels[part] = made[:, part * BREADTH : (part + 1) * BREADTH]

    gap = (iota((PATCH, slots), 0) + 1).astype(F32) - row_start
    row_weight = jnp.zeros((PATCH, slots), F32)
    for k in range(4):
        inside = (gap >= k) & (gap < HEIGHT + k)
        row_weight = row_weight + jnp.where(inside, row_taps[k], 0.0)
    gap = (iota((slots, PATCH), 1) + 1).astype(F32) - table[:, at + 10 : at + 11]
    col_weight = jnp.zeros((slots, PATCH), F32)
    for k in range(4):
        inside = (gap >= k) & (gap < BREADTH + k)
        col_weight = col_weight + jnp.where(inside, table[:, at + 4 + k : at + 5 + k], 0.0)
    row_high = row_weight.astype(BF16)
    row_low = (row_weight - row_high.astype(F32)).astype(BF16)
    col_high = col_weight.astype(BF16)
    col_low = (col_weight - col_high.astype(F32)).astype(BF16)
    depth = dot(row_high, col_high) + (dot(row_high, col_low) + dot(row_low, col_high))
    shares = PATCH // HEIGHT
    for v in range(shares):
        out[v, HEIGHT:, :] = depth[v * HEIGHT : (v + 1) * HEIGHT, :].astype(out.dtype)

    for copy in copies:
        copy.wait()

    sums = (sum_a, sum_b, sum_c, sum_d)
    for ref in sums + (padded_a, padded_b):
        ref[...] = jnp.zeros_like(ref)
    lane = iota((HEIGHT, BREADTH), 1)
    line = iota((8, BREADTH), 1)
    apart = (lane & (HEIGHT - 1)) - iota((HEIGHT, BREADTH), 0)
    near_row = (apart <= REACH) & (apart >= -REACH)
    nothing = jnp.zeros((HEIGHT, BREADTH), BF16)
    per_cap = sources // GROUP

    def tall(x):
        return jnp.concatenate([x] * (WINDOW // 8), axis=0)

    def build(g, q, left, shifted):
        k = g // per_cap
        first = (g - k * per_cap) * GROUP
        pixels = blocks[first + q, pl.ds(pl.multiple_of(k * HEIGHT, HEIGHT), HEIGHT), :]
        for outer in range(OUTER):
            at = pl.ds(outer * HEIGHT, HEIGHT)
            move = REACH - 1 - INNER * outer
            if move == 0:
                shifted[q, at, :BREADTH] = pixels
                continue
            moved = pltpu.roll(pixels, move % BREADTH, 1)
            kept = lane >= move if move > 0 else lane < BREADTH + move
            shifted[q, at, :BREADTH] = jnp.where(kept, moved, nothing)
            shifted[q, at, BREADTH:] = jnp.where(kept, nothing, moved)
        for inner in range(INNER):
            for half in range(2):
                row = kernels[2 * inner + half, pl.ds(g * GROUP + q, 1), :]
                turn = pltpu.roll(
                    jnp.broadcast_to(row, (HEIGHT, BREADTH)), 0, 1, stride=1, stride_axis=0
                )
                left[q, pl.ds(inner * HEIGHT, HEIGHT), half * BREADTH : (half + 1) * BREADTH] = jnp.where(
                    near_row, turn, 0.0
                ).astype(BF16)

    def convolve(q, left, shifted, padded):
        product = dot(left[q], shifted[q])
        before, centre, after = (product[inner * HEIGHT : (inner + 1) * HEIGHT, :] for inner in range(INNER))
        before = jnp.where(lane == BREADTH - 1, before[:, BREADTH:], before[:, :BREADTH])
        after = jnp.where(lane == 0, after[:, BREADTH:], after[:, :BREADTH])
        total = centre[:, :BREADTH] + pltpu.roll(before, 1, 1) + pltpu.roll(after, BREADTH - 1, 1)
        padded[q, pl.ds(8, HEIGHT), :] = total.astype(BF16).astype(F32)

    def resample(g, q, padded):
        s = g * GROUP + q
        row_at = whole_s[0, s]
        col_at = whole_s[1, s]
        tapped = fields_s[0, s] * padded[q, pl.ds(8, WINDOW), :]
        for t in range(1, 4):
            tapped = tapped + fields_s[t, s] * padded[q, pl.ds(8 - t, WINDOW), :]
        wide_low = wide_all = None
        for t in range(4):
            tap = fields_s[4 + t, s]
            if t == 0:
                tap = tall(jnp.where((line == BREADTH - 1) & (col_at == 0), 0.0, tap))
            if t == 3:
                tap = tall(jnp.where((line == 0) & (col_at == BREADTH - 1), 0.0, tap))
            term = tap * pltpu.roll(tapped, lax.rem(col_at + (BREADTH + t - 1), BREADTH), 1)
            wide_all = term if t == 0 else wide_all + term
            begun = tall(line >= col_at + (t - 1))
            wide_low = jnp.where(begun, wide_all, 0.0 if t == 0 else wide_low)
        wide_high = wide_all - wide_low
        low, high = sums[2 * (q % 2)], sums[2 * (q % 2) + 1]
        low[pl.ds(row_at + 7, WINDOW), :] += wide_low
        high[pl.ds(row_at + 7, WINDOW), :] += wide_high

    used = OUTER * HEIGHT
    still = pl.ds((OUTER // 2) * HEIGHT, HEIGHT)
    for ref in (shifted_a, shifted_b):
        ref[:, used:, :] = jnp.zeros((GROUP, PATCH - used, PATCH), BF16)
        ref[:, still, BREADTH:] = jnp.zeros((GROUP, HEIGHT, BREADTH), BF16)
    for q in range(GROUP):
        build(0, q, left_a, shifted_a)

    def work(h, carry):
        g = 2 * h
        for q in range(GROUP):
            convolve(q, left_a, shifted_a, padded_a)
            build(g + 1, q, left_b, shifted_b)
            resample(jnp.maximum(g - 1, 0), q, padded_b)
        for q in range(GROUP):
            convolve(q, left_b, shifted_b, padded_b)
            build(jnp.minimum(g + 2, groups - 1), q, left_a, shifted_a)
            resample(g, q, padded_a)
        return carry

    lax.fori_loop(0, groups // 2, work, 0)
    for q in range(GROUP):
        resample(groups - 1, q, padded_b)
    for v in range(shares):
        rows = pl.ds(8 + v * HEIGHT, HEIGHT)
        for half in range(2):
            both = sums[half][rows, :] + sums[2 + half][rows, :]
            out[v, :HEIGHT, half * BREADTH : (half + 1) * BREADTH] = both.astype(out.dtype)


def coadd_sums(blocks):
    sources = blocks.shape[0]
    slots = CAP * sources
    vmem = pl.BlockSpec(memory_space=pltpu.VMEM)
    return pl.pallas_call(
        functools.partial(coadd_body, sources),
        out_shape=jax.ShapeDtypeStruct((PATCH // HEIGHT, 2 * HEIGHT, PATCH), BF16),
        in_specs=[vmem],
        out_specs=vmem,
        scratch_shapes=[
            pltpu.VMEM((sources * TAIL, BREADTH), F32),
            pltpu.VMEM((slots, BREADTH), F32),
            pltpu.VMEM((2 * INNER, slots, BREADTH), F32),
            pltpu.VMEM((GROUP, INNER * HEIGHT, PATCH), BF16),
            pltpu.VMEM((GROUP, INNER * HEIGHT, PATCH), BF16),
            pltpu.VMEM((GROUP, PATCH, PATCH), BF16),
            pltpu.VMEM((GROUP, PATCH, PATCH), BF16),
            pltpu.VMEM((GROUP, 8 + HEIGHT + 8, BREADTH), F32),
            pltpu.VMEM((GROUP, 8 + HEIGHT + 8, BREADTH), F32),
            pltpu.VMEM((PATCH + 16, BREADTH), F32),
            pltpu.VMEM((PATCH + 16, BREADTH), F32),
            pltpu.VMEM((PATCH + 16, BREADTH), F32),
            pltpu.VMEM((PATCH + 16, BREADTH), F32),
            pltpu.VMEM((8, slots), F32),
            pltpu.VMEM((8, slots), jnp.int32),
            pltpu.SMEM((8, slots), F32),
            pltpu.SMEM((8, slots), jnp.int32),
            pltpu.SemaphoreType.DMA((2,)),
        ],
        compiler_params=pltpu.CompilerParams(vmem_limit_bytes=48 << 20),
        name="coadd",
    )(blocks)


def finish_body(sums, coadd, depth_map):
    total = sums[0].astype(F32)
    for v in range(1, sums.shape[0]):
        total = total + sums[v].astype(F32)
    depth = total[HEIGHT:, :]
    depth_map[...] = depth
    coadd[...] = total[:HEIGHT, :] / (1.0 + depth)


def finish(sums):
    vmem = pl.BlockSpec(memory_space=pltpu.VMEM)
    return pl.pallas_call(
        finish_body,
        out_shape=[jax.ShapeDtypeStruct((HEIGHT, PATCH), F32)] * 2,
        in_specs=[vmem],
        out_specs=[vmem, vmem],
        compiler_params=pltpu.CompilerParams(vmem_limit_bytes=4 << 20),
        name="finish",
    )(sums)


def per_device(stamps, coefs, basis, taps, weights, target, row_offset, col_offset):
    places = lax.axis_size("patch")
    blocks = pack(
        target[:, :, 0], stamps[0], coefs[0].T, basis[0, 0], taps[0].T, weights, row_offset, col_offset, places
    )
    blocks = lax.all_to_all(blocks, "patch", split_axis=0, concat_axis=0, tiled=True)
    sums = coadd_sums(blocks)
    sums = lax.all_to_all(sums, "visit", split_axis=0, concat_axis=0, tiled=True)
    coadd, depth_map = finish(sums)
    return (coadd[None], depth_map[None])


def solution(mesh):
    placed = (
        P("visit", "patch", None, None),
        P("visit", "patch", None),
        P("visit", "patch", None, None),
        P("visit", "patch", None),
        P("visit", "patch"),
        P("visit", "patch", None),
        P("visit", "patch"),
        P("visit", "patch"),
    )
    return jax.shard_map(
        per_device,
        mesh=mesh,
        in_specs=placed,
        out_specs=(P("patch", "visit", None), P("patch", "visit", None)),
        check_vma=False,
    )
```

```python
import functools

import jax
import jax.numpy as jnp
from jax import lax
from jax.experimental import pallas as pl
from jax.experimental.pallas import tpu as pltpu
from jax.sharding import PartitionSpec as P

BF16 = jnp.bfloat16
F32 = jnp.float32
KERNEL = 21
REACH = 10
TERMS = 64
HEIGHT = 32
BREADTH = 128
PATCH = 256
CAP = 4
TAIL = 8
BLOCK_ROWS = CAP * HEIGHT + TAIL
INNER = 3
OUTER = 7
WINDOW = HEIGHT + 8
GROUP = 8
OPERANDS = 9
SIDE = 6


def iota(shape, axis):
    return lax.broadcasted_iota(jnp.int32, shape, axis)


def dot(a, b):
    return jnp.dot(a, b, preferred_element_type=F32)


def pack_body(*refs):
    given, out, here, count, sem = refs[:OPERANDS], refs[OPERANDS], refs[OPERANDS + 1 : -2], refs[-2], refs[-1]
    target_s, target, coefs, basis, taps, weights, row_offset, col_offset, held = here
    places = out.shape[0]
    stamp_count = held.shape[0]
    fetches = [
        pltpu.make_async_copy(source, place, sem.at[n]) for n, (source, place) in enumerate(zip(given, here))
    ]
    for fetch in fetches:
        fetch.start()
    out[...] = jnp.zeros_like(out)
    for fetch in fetches[:-1]:
        fetch.wait()
    across = jnp.broadcast_to(target[...].astype(F32), (stamp_count, stamp_count))
    square = (stamp_count, stamp_count)
    earlier = (across.T == across) & (iota(square, 0) < iota(square, 1))
    rank = jnp.sum(jnp.where(earlier, 1.0, 0.0), axis=0, keepdims=True)
    place = target[...] * TAIL + (TAIL - CAP) + rank.astype(jnp.int32)
    chosen = jnp.where(iota((places * TAIL, stamp_count), 0) == place, 1.0, 0.0).astype(BF16)
    extras = jnp.concatenate(
        [
            coefs[...].astype(F32),
            taps[...].astype(F32),
            weights[...].astype(F32),
            row_offset[...].astype(F32),
            col_offset[...].astype(F32),
            jnp.zeros((BREADTH - TERMS - 11, stamp_count), F32),
        ],
        axis=0,
    )
    tail = lax.dot_general(
        chosen, extras.astype(BF16), (((1,), (1,)), ((), ())), preferred_element_type=F32
    )
    wide = jnp.pad(basis[...].astype(F32), ((0, 24 - KERNEL), (0, BREADTH - KERNEL)))
    seat = iota(wide.shape, 0)
    seat = seat - SIDE * ((seat * 11) >> 6)
    laid = jnp.where(seat == 0, wide, 0.0)
    for r in range(1, SIDE):
        laid = laid + jnp.where(seat == r, pltpu.roll(wide, r * KERNEL, 1), 0.0)
    fold = jnp.where((iota((TAIL, 24), 1) * 11) >> 6 == iota((TAIL, 24), 0), 1.0, 0.0)
    shared = dot(fold.astype(BF16), laid.astype(BF16))
    tail = tail.reshape(places, TAIL, BREADTH) + shared[None]
    out[:, CAP * HEIGHT :, :] = tail.astype(BF16)

    def clear(d, carry):
        count[d] = 0
        return carry

    lax.fori_loop(0, places, clear, 0, unroll=8)
    fetches[-1].wait()

    def put(s, carry):
        d = target_s[0, s]
        k = count[d]
        count[d] = k + 1
        out[d, pl.ds(pl.multiple_of(k * HEIGHT, HEIGHT), HEIGHT), :] = held[s]
        return carry

    lax.fori_loop(0, stamp_count, put, 0, unroll=4)


def pack(target, stamps, coefs, basis, taps, weights, row_offset, col_offset, places):
    given = (target, target, coefs, basis, taps, weights, row_offset, col_offset, stamps)
    here = [pltpu.SMEM(target.shape, jnp.int32)] + [pltpu.VMEM(x.shape, x.dtype) for x in given[1:]]
    return pl.pallas_call(
        pack_body,
        out_shape=jax.ShapeDtypeStruct((places, BLOCK_ROWS, BREADTH), BF16),
        in_specs=[pl.BlockSpec(memory_space=pltpu.HBM)] * OPERANDS,
        out_specs=pl.BlockSpec(memory_space=pltpu.VMEM),
        scratch_shapes=here + [pltpu.SMEM((places,), jnp.int32), pltpu.SemaphoreType.DMA((OPERANDS,))],
        compiler_params=pltpu.CompilerParams(vmem_limit_bytes=40 << 20),
        name="pack",
    )(*(pltpu.with_memory_space_constraint(x, pltpu.HBM) for x in given))


def coadd_body(
    sources, blocks, out, tail, meta, kernels, left_a, left_b, shifted_a, shifted_b, padded_a, padded_b,
    sum_a, sum_b, sum_c, sum_d, fields, whole, fields_s, whole_s, listed, sem
):
    slots = CAP * sources
    bits = sources.bit_length() - 1
    tail[...] = blocks[:, CAP * HEIGHT :, :].astype(F32).reshape(sources * TAIL, BREADTH)
    basis = jnp.concatenate(
        [tail[pl.ds(q, sources, stride=TAIL), :] for q in range(TAIL - CAP)], axis=1
    ).astype(BF16)
    for k in range(CAP):
        meta[pl.ds(k * sources, sources), :] = tail[pl.ds(TAIL - CAP + k, sources, stride=TAIL), :]
    table = meta[...]
    coefs = table[:, :TERMS].astype(BF16)

    turned = table.T
    at = TERMS
    weight = turned[at + 8 : at + 9, :]
    row_start = turned[at + 9 : at + 10, :]
    row_taps = [
        (weight * turned[at + k : at + k + 1, :]).astype(BF16).astype(F32) for k in range(4)
    ]
    fields[...] = jnp.concatenate(row_taps + [turned[at + 4 : at + 8, :]], axis=0)
    whole[...] = jnp.concatenate(
        [turned[at + 9 : at + 11, :], jnp.where(weight != 0.0, 1.0, 0.0), jnp.zeros((5, slots), F32)], axis=0
    ).astype(jnp.int32)
    copies = [
        pltpu.make_async_copy(fields, fields_s, sem.at[0]),
        pltpu.make_async_copy(whole, whole_s, sem.at[1]),
    ]
    for copy in copies:
        copy.start()

    flat = iota((4 * BREADTH, 1), 0)
    seat = flat & (BREADTH - 1)
    turn = (seat * 3121) >> 16
    a = (flat >> 7) * SIDE + turn
    b = seat - turn * KERNEL
    outer = (b * 11) >> 5
    there = (b - INNER * outer) * PATCH + (outer >> 2) * BREADTH
    there = there + ((outer * HEIGHT + a - REACH) & (BREADTH - 1))
    there = jnp.where((turn < SIDE) & (a < KERNEL), there, -1)
    moved = jnp.where(iota((4 * BREADTH, INNER * PATCH), 1) == there, 1.0, 0.0).astype(BF16)
    arranged = dot(basis, moved).astype(BF16)
    made = dot(coefs, arranged).astype(BF16).astype(F32)
    for part in range(2 * INNER):
        kernels[part] = made[:, part * BREADTH : (part + 1) * BREADTH]

    gap = (iota((PATCH, slots), 0) + 1).astype(F32) - row_start
    row_weight = jnp.zeros((PATCH, slots), F32)
    for k in range(4):
        inside = (gap >= k) & (gap < HEIGHT + k)
        row_weight = row_weight + jnp.where(inside, row_taps[k], 0.0)
    gap = (iota((slots, PATCH), 1) + 1).astype(F32) - table[:, at + 10 : at + 11]
    col_weight = jnp.zeros((slots, PATCH), F32)
    for k in range(4):
        inside = (gap >= k) & (gap < BREADTH + k)
        col_weight = col_weight + jnp.where(inside, table[:, at + 4 + k : at + 5 + k], 0.0)
    row_high = row_weight.astype(BF16)
    row_low = (row_weight - row_high.astype(F32)).astype(BF16)
    col_high = col_weight.astype(BF16)
    col_low = (col_weight - col_high.astype(F32)).astype(BF16)
    depth = dot(row_high, col_high) + (dot(row_high, col_low) + dot(row_low, col_high))
    shares = PATCH // HEIGHT
    for v in range(shares):
        out[v, HEIGHT:, :] = depth[v * HEIGHT : (v + 1) * HEIGHT, :].astype(out.dtype)

    for copy in copies:
        copy.wait()

    sums = (sum_a, sum_b, sum_c, sum_d)
    for ref in sums + (padded_a, padded_b):
        ref[...] = jnp.zeros_like(ref)
    lane = iota((HEIGHT, BREADTH), 1)
    line = iota((8, BREADTH), 1)
    apart = (lane & (HEIGHT - 1)) - iota((HEIGHT, BREADTH), 0)
    near_row = (apart <= REACH) & (apart >= -REACH)
    nothing = jnp.zeros((HEIGHT, BREADTH), BF16)

    def tall(x):
        return jnp.concatenate([x] * (WINDOW // 8), axis=0)

    def build(g, q, left, shifted):
        s = listed[g * GROUP + q]
        k = s >> bits
        pixels = blocks[s - (k << bits), pl.ds(pl.multiple_of(k * HEIGHT, HEIGHT), HEIGHT), :]
        for outer in range(OUTER):
            at = pl.ds(outer * HEIGHT, HEIGHT)
            move = REACH - 1 - INNER * outer
            if move == 0:
                shifted[q, at, :BREADTH] = pixels
                continue
            moved = pltpu.roll(pixels, move % BREADTH, 1)
            kept = lane >= move if move > 0 else lane < BREADTH + move
            shifted[q, at, :BREADTH] = jnp.where(kept, moved, nothing)
            shifted[q, at, BREADTH:] = jnp.where(kept, nothing, moved)
        for inner in range(INNER):
            for half in range(2):
                row = kernels[2 * inner + half, pl.ds(s, 1), :]
                turn = pltpu.roll(
                    jnp.broadcast_to(row, (HEIGHT, BREADTH)), 0, 1, stride=1, stride_axis=0
                )
                left[q, pl.ds(inner * HEIGHT, HEIGHT), half * BREADTH : (half + 1) * BREADTH] = jnp.where(
                    near_row, turn, 0.0
                ).astype(BF16)

    def convolve(q, left, shifted, padded):
        product = dot(left[q], shifted[q])
        before, centre, after = (product[inner * HEIGHT : (inner + 1) * HEIGHT, :] for inner in range(INNER))
        before = jnp.where(lane == BREADTH - 1, before[:, BREADTH:], before[:, :BREADTH])
        after = jnp.where(lane == 0, after[:, BREADTH:], after[:, :BREADTH])
        total = centre[:, :BREADTH] + pltpu.roll(before, 1, 1) + pltpu.roll(after, BREADTH - 1, 1)
        padded[q, pl.ds(8, HEIGHT), :] = total.astype(BF16).astype(F32)

    def resample(g, q, padded):
        s = listed[g * GROUP + q]
        row_at = whole_s[0, s]
        col_at = whole_s[1, s]
        tapped = fields_s[0, s] * padded[q, pl.ds(8, WINDOW), :]
        for t in range(1, 4):
            tapped = tapped + fields_s[t, s] * padded[q, pl.ds(8 - t, WINDOW), :]
        wide_low = wide_all = None
        for t in range(4):
            tap = fields_s[4 + t, s]
            if t == 0:
                tap = tall(jnp.where((line == BREADTH - 1) & (col_at == 0), 0.0, tap))
            if t == 3:
                tap = tall(jnp.where((line == 0) & (col_at == BREADTH - 1), 0.0, tap))
            term = tap * pltpu.roll(tapped, lax.rem(col_at + (BREADTH + t - 1), BREADTH), 1)
            wide_all = term if t == 0 else wide_all + term
            begun = tall(line >= col_at + (t - 1))
            wide_low = jnp.where(begun, wide_all, 0.0 if t == 0 else wide_low)
        wide_high = wide_all - wide_low
        low, high = sums[2 * (q % 2)], sums[2 * (q % 2) + 1]
        low[pl.ds(row_at + 7, WINDOW), :] += wide_low
        high[pl.ds(row_at + 7, WINDOW), :] += wide_high

    used = OUTER * HEIGHT
    still = pl.ds((OUTER // 2) * HEIGHT, HEIGHT)
    for ref in (shifted_a, shifted_b):
        ref[:, used:, :] = jnp.zeros((GROUP, PATCH - used, PATCH), BF16)
        ref[:, still, BREADTH:] = jnp.zeros((GROUP, HEIGHT, BREADTH), BF16)
    def note(s, carry):
        number, empty = carry
        holds = whole_s[2, s]
        listed[number] = s
        return number + holds, jnp.where(holds == 0, s, empty)

    number, empty = lax.fori_loop(0, slots, note, (0, 0), unroll=16)

    def fill(n, carry):
        listed[number + n] = empty
        return carry

    lax.fori_loop(0, 2 * GROUP, fill, 0, unroll=4)
    rounds = jnp.maximum((number + 2 * GROUP - 1) // (2 * GROUP), 1)
    groups = 2 * rounds
    for q in range(GROUP):
        build(0, q, left_a, shifted_a)

    def work(h, carry):
        g = 2 * h
        for q in range(GROUP):
            convolve(q, left_a, shifted_a, padded_a)
            build(g + 1, q, left_b, shifted_b)
            resample(jnp.maximum(g - 1, 0), q, padded_b)
        for q in range(GROUP):
            convolve(q, left_b, shifted_b, padded_b)
            build(jnp.minimum(g + 2, groups - 1), q, left_a, shifted_a)
            resample(g, q, padded_a)
        return carry

    lax.fori_loop(0, rounds, work, 0)
    for q in range(GROUP):
        resample(groups - 1, q, padded_b)
    for v in range(shares):
        rows = pl.ds(8 + v * HEIGHT, HEIGHT)
        for half in range(2):
            both = sums[half][rows, :] + sums[2 + half][rows, :]
            out[v, :HEIGHT, half * BREADTH : (half + 1) * BREADTH] = both.astype(out.dtype)


def coadd_sums(blocks):
    sources = blocks.shape[0]
    slots = CAP * sources
    vmem = pl.BlockSpec(memory_space=pltpu.VMEM)
    return pl.pallas_call(
        functools.partial(coadd_body, sources),
        out_shape=jax.ShapeDtypeStruct((PATCH // HEIGHT, 2 * HEIGHT, PATCH), BF16),
        in_specs=[vmem],
        out_specs=vmem,
        scratch_shapes=[
            pltpu.VMEM((sources * TAIL, BREADTH), F32),
            pltpu.VMEM((slots, BREADTH), F32),
            pltpu.VMEM((2 * INNER, slots, BREADTH), F32),
            pltpu.VMEM((GROUP, INNER * HEIGHT, PATCH), BF16),
            pltpu.VMEM((GROUP, INNER * HEIGHT, PATCH), BF16),
            pltpu.VMEM((GROUP, PATCH, PATCH), BF16),
            pltpu.VMEM((GROUP, PATCH, PATCH), BF16),
            pltpu.VMEM((GROUP, 8 + HEIGHT + 8, BREADTH), F32),
            pltpu.VMEM((GROUP, 8 + HEIGHT + 8, BREADTH), F32),
            pltpu.VMEM((PATCH + 16, BREADTH), F32),
            pltpu.VMEM((PATCH + 16, BREADTH), F32),
            pltpu.VMEM((PATCH + 16, BREADTH), F32),
            pltpu.VMEM((PATCH + 16, BREADTH), F32),
            pltpu.VMEM((8, slots), F32),
            pltpu.VMEM((8, slots), jnp.int32),
            pltpu.SMEM((8, slots), F32),
            pltpu.SMEM((8, slots), jnp.int32),
            pltpu.SMEM((slots + 2 * GROUP,), jnp.int32),
            pltpu.SemaphoreType.DMA((2,)),
        ],
        compiler_params=pltpu.CompilerParams(vmem_limit_bytes=48 << 20),
        name="coadd",
    )(blocks)


def finish_body(sums, coadd, depth_map):
    total = sums[0].astype(F32)
    for v in range(1, sums.shape[0]):
        total = total + sums[v].astype(F32)
    depth = total[HEIGHT:, :]
    depth_map[...] = depth
    coadd[...] = total[:HEIGHT, :] / (1.0 + depth)


def finish(sums):
    vmem = pl.BlockSpec(memory_space=pltpu.VMEM)
    return pl.pallas_call(
        finish_body,
        out_shape=[jax.ShapeDtypeStruct((HEIGHT, PATCH), F32)] * 2,
        in_specs=[vmem],
        out_specs=[vmem, vmem],
        compiler_params=pltpu.CompilerParams(vmem_limit_bytes=4 << 20),
        name="finish",
    )(sums)


def per_device(stamps, coefs, basis, taps, weights, target, row_offset, col_offset):
    places = lax.axis_size("patch")
    blocks = pack(
        target[:, :, 0], stamps[0], coefs[0].T, basis[0, 0], taps[0].T, weights, row_offset, col_offset, places
    )
    blocks = lax.all_to_all(blocks, "patch", split_axis=0, concat_axis=0, tiled=True)
    sums = coadd_sums(blocks)
    sums = lax.all_to_all(sums, "visit", split_axis=0, concat_axis=0, tiled=True)
    coadd, depth_map = finish(sums)
    return (coadd[None], depth_map[None])


def solution(mesh):
    placed = (
        P("visit", "patch", None, None),
        P("visit", "patch", None),
        P("visit", "patch", None, None),
        P("visit", "patch", None),
        P("visit", "patch"),
        P("visit", "patch", None),
        P("visit", "patch"),
        P("visit", "patch"),
    )
    return jax.shard_map(
        per_device,
        mesh=mesh,
        in_specs=placed,
        out_specs=(P("patch", "visit", None), P("patch", "visit", None)),
        check_vma=False,
    )
```

```python
import functools

import jax
import jax.numpy as jnp
from jax import lax
from jax.experimental import pallas as pl
from jax.experimental.pallas import tpu as pltpu
from jax.sharding import PartitionSpec as P

BF16 = jnp.bfloat16
F32 = jnp.float32
KERNEL = 21
REACH = 10
TERMS = 64
HEIGHT = 32
BREADTH = 128
PATCH = 256
CAP = 4
TAIL = 8
BLOCK_ROWS = CAP * HEIGHT + TAIL
INNER = 3
OUTER = 7
WINDOW = HEIGHT + 8
GROUP = 8
OPERANDS = 9
SIDE = 6


def iota(shape, axis):
    return lax.broadcasted_iota(jnp.int32, shape, axis)


def dot(a, b):
    return jnp.dot(a, b, preferred_element_type=F32)


def pack_body(*refs):
    given, out, here, count, sem = refs[:OPERANDS], refs[OPERANDS], refs[OPERANDS + 1 : -2], refs[-2], refs[-1]
    target_s, target, coefs, basis, taps, weights, row_offset, col_offset, held = here
    places = out.shape[0]
    stamp_count = held.shape[0]
    fetches = [
        pltpu.make_async_copy(source, place, sem.at[n]) for n, (source, place) in enumerate(zip(given, here))
    ]
    for fetch in fetches:
        fetch.start()
    out[...] = jnp.zeros_like(out)
    for fetch in fetches[:-1]:
        fetch.wait()
    across = jnp.broadcast_to(target[...].astype(F32), (stamp_count, stamp_count))
    square = (stamp_count, stamp_count)
    earlier = (across.T == across) & (iota(square, 0) < iota(square, 1))
    rank = jnp.sum(jnp.where(earlier, 1.0, 0.0), axis=0, keepdims=True)
    place = target[...] * TAIL + (TAIL - CAP) + rank.astype(jnp.int32)
    chosen = jnp.where(iota((places * TAIL, stamp_count), 0) == place, 1.0, 0.0).astype(BF16)
    extras = jnp.concatenate(
        [
            coefs[...].astype(F32),
            taps[...].astype(F32),
            weights[...].astype(F32),
            row_offset[...].astype(F32),
            col_offset[...].astype(F32),
            jnp.zeros((BREADTH - TERMS - 11, stamp_count), F32),
        ],
        axis=0,
    )
    tail = lax.dot_general(
        chosen, extras.astype(BF16), (((1,), (1,)), ((), ())), preferred_element_type=F32
    )
    wide = jnp.pad(basis[...].astype(F32), ((0, 24 - KERNEL), (0, BREADTH - KERNEL)))
    seat = iota(wide.shape, 0)
    seat = seat - SIDE * ((seat * 11) >> 6)
    laid = jnp.where(seat == 0, wide, 0.0)
    for r in range(1, SIDE):
        laid = laid + jnp.where(seat == r, pltpu.roll(wide, r * KERNEL, 1), 0.0)
    fold = jnp.where((iota((TAIL, 24), 1) * 11) >> 6 == iota((TAIL, 24), 0), 1.0, 0.0)
    shared = dot(fold.astype(BF16), laid.astype(BF16))
    tail = tail.reshape(places, TAIL, BREADTH) + shared[None]
    out[:, CAP * HEIGHT :, :] = tail.astype(BF16)

    def clear(d, carry):
        count[d] = 0
        return carry

    lax.fori_loop(0, places, clear, 0, unroll=8)
    fetches[-1].wait()

    def put(s, carry):
        d = target_s[0, s]
        k = count[d]
        count[d] = k + 1
        out[d, pl.ds(pl.multiple_of(k * HEIGHT, HEIGHT), HEIGHT), :] = held[s]
        return carry

    lax.fori_loop(0, stamp_count, put, 0, unroll=8)


def pack(target, stamps, coefs, basis, taps, weights, row_offset, col_offset, places):
    given = (target, target, coefs, basis, taps, weights, row_offset, col_offset, stamps)
    here = [pltpu.SMEM(target.shape, jnp.int32)] + [pltpu.VMEM(x.shape, x.dtype) for x in given[1:]]
    return pl.pallas_call(
        pack_body,
        out_shape=jax.ShapeDtypeStruct((places, BLOCK_ROWS, BREADTH), BF16),
        in_specs=[pl.BlockSpec(memory_space=pltpu.HBM)] * OPERANDS,
        out_specs=pl.BlockSpec(memory_space=pltpu.VMEM),
        scratch_shapes=here + [pltpu.SMEM((places,), jnp.int32), pltpu.SemaphoreType.DMA((OPERANDS,))],
        compiler_params=pltpu.CompilerParams(vmem_limit_bytes=40 << 20),
        name="pack",
    )(*(pltpu.with_memory_space_constraint(x, pltpu.HBM) for x in given))


def coadd_body(
    sources, blocks, out, tail, meta, kernels, left_a, left_b, shifted_a, shifted_b, padded_a, padded_b,
    sum_a, sum_b, sum_c, sum_d, fields, whole, fields_s, whole_s, listed, sem
):
    slots = CAP * sources
    bits = sources.bit_length() - 1
    tail[...] = blocks[:, CAP * HEIGHT :, :].astype(F32).reshape(sources * TAIL, BREADTH)
    basis = jnp.concatenate(
        [tail[pl.ds(q, sources, stride=TAIL), :] for q in range(TAIL - CAP)], axis=1
    ).astype(BF16)
    for k in range(CAP):
        meta[pl.ds(k * sources, sources), :] = tail[pl.ds(TAIL - CAP + k, sources, stride=TAIL), :]
    table = meta[...]
    coefs = table[:, :TERMS].astype(BF16)

    turned = table.T
    at = TERMS
    weight = turned[at + 8 : at + 9, :]
    row_start = turned[at + 9 : at + 10, :]
    row_taps = [
        (weight * turned[at + k : at + k + 1, :]).astype(BF16).astype(F32) for k in range(4)
    ]
    fields[...] = jnp.concatenate(row_taps + [turned[at + 4 : at + 8, :]], axis=0)
    whole[...] = jnp.concatenate(
        [turned[at + 9 : at + 11, :], jnp.where(weight != 0.0, 1.0, 0.0), jnp.zeros((5, slots), F32)], axis=0
    ).astype(jnp.int32)
    copies = [
        pltpu.make_async_copy(fields, fields_s, sem.at[0]),
        pltpu.make_async_copy(whole, whole_s, sem.at[1]),
    ]
    for copy in copies:
        copy.start()

    flat = iota((4 * BREADTH, 1), 0)
    seat = flat & (BREADTH - 1)
    turn = (seat * 3121) >> 16
    a = (flat >> 7) * SIDE + turn
    b = seat - turn * KERNEL
    outer = (b * 11) >> 5
    there = (b - INNER * outer) * PATCH + (outer >> 2) * BREADTH
    there = there + ((outer * HEIGHT + a - REACH) & (BREADTH - 1))
    there = jnp.where((turn < SIDE) & (a < KERNEL), there, -1)
    moved = jnp.where(iota((4 * BREADTH, INNER * PATCH), 1) == there, 1.0, 0.0).astype(BF16)
    arranged = dot(basis, moved).astype(BF16)
    made = dot(coefs, arranged).astype(BF16).astype(F32)
    for part in range(2 * INNER):
        kernels[part] = made[:, part * BREADTH : (part + 1) * BREADTH]

    gap = (iota((PATCH, slots), 0) + 1).astype(F32) - row_start
    row_weight = jnp.zeros((PATCH, slots), F32)
    for k in range(4):
        inside = (gap >= k) & (gap < HEIGHT + k)
        row_weight = row_weight + jnp.where(inside, row_taps[k], 0.0)
    gap = (iota((slots, PATCH), 1) + 1).astype(F32) - table[:, at + 10 : at + 11]
    col_weight = jnp.zeros((slots, PATCH), F32)
    for k in range(4):
        inside = (gap >= k) & (gap < BREADTH + k)
        col_weight = col_weight + jnp.where(inside, table[:, at + 4 + k : at + 5 + k], 0.0)
    row_high = row_weight.astype(BF16)
    row_low = (row_weight - row_high.astype(F32)).astype(BF16)
    col_high = col_weight.astype(BF16)
    col_low = (col_weight - col_high.astype(F32)).astype(BF16)
    depth = dot(row_high, col_high) + (dot(row_high, col_low) + dot(row_low, col_high))
    shares = PATCH // HEIGHT
    for v in range(shares):
        out[v, HEIGHT:, :] = depth[v * HEIGHT : (v + 1) * HEIGHT, :].astype(out.dtype)

    for copy in copies:
        copy.wait()

    sums = (sum_a, sum_b, sum_c, sum_d)
    for ref in sums + (padded_a, padded_b):
        ref[...] = jnp.zeros_like(ref)
    lane = iota((HEIGHT, BREADTH), 1)
    line = iota((8, BREADTH), 1)
    apart = (lane & (HEIGHT - 1)) - iota((HEIGHT, BREADTH), 0)
    near_row = (apart <= REACH) & (apart >= -REACH)
    nothing = jnp.zeros((HEIGHT, BREADTH), BF16)

    def tall(x):
        return jnp.concatenate([x] * (WINDOW // 8), axis=0)

    def build(g, q, left, shifted):
        s = listed[g * GROUP + q]
        k = s >> bits
        pixels = blocks[s - (k << bits), pl.ds(pl.multiple_of(k * HEIGHT, HEIGHT), HEIGHT), :]
        for outer in range(OUTER):
            at = pl.ds(outer * HEIGHT, HEIGHT)
            move = REACH - 1 - INNER * outer
            if move == 0:
                shifted[q, at, :BREADTH] = pixels
                continue
            moved = pltpu.roll(pixels, move % BREADTH, 1)
            kept = lane >= move if move > 0 else lane < BREADTH + move
            shifted[q, at, :BREADTH] = jnp.where(kept, moved, nothing)
            shifted[q, at, BREADTH:] = jnp.where(kept, nothing, moved)
        for inner in range(INNER):
            for half in range(2):
                row = kernels[2 * inner + half, pl.ds(s, 1), :]
                turn = pltpu.roll(
                    jnp.broadcast_to(row, (HEIGHT, BREADTH)), 0, 1, stride=1, stride_axis=0
                )
                left[q, pl.ds(inner * HEIGHT, HEIGHT), half * BREADTH : (half + 1) * BREADTH] = jnp.where(
                    near_row, turn, 0.0
                ).astype(BF16)

    def convolve(q, left, shifted, padded):
        product = dot(left[q], shifted[q])
        before, centre, after = (product[inner * HEIGHT : (inner + 1) * HEIGHT, :] for inner in range(INNER))
        before = jnp.where(lane == BREADTH - 1, before[:, BREADTH:], before[:, :BREADTH])
        after = jnp.where(lane == 0, after[:, BREADTH:], after[:, :BREADTH])
        total = centre[:, :BREADTH] + pltpu.roll(before, 1, 1) + pltpu.roll(after, BREADTH - 1, 1)
        padded[q, pl.ds(8, HEIGHT), :] = total.astype(BF16).astype(F32)

    def resample(g, q, padded):
        s = listed[g * GROUP + q]
        row_at = whole_s[0, s]
        col_at = whole_s[1, s]
        tapped = fields_s[0, s] * padded[q, pl.ds(8, WINDOW), :]
        for t in range(1, 4):
            tapped = tapped + fields_s[t, s] * padded[q, pl.ds(8 - t, WINDOW), :]
        wide_low = wide_all = None
        for t in range(4):
            tap = fields_s[4 + t, s]
            if t == 0:
                tap = tall(jnp.where((line == BREADTH - 1) & (col_at == 0), 0.0, tap))
            if t == 3:
                tap = tall(jnp.where((line == 0) & (col_at == BREADTH - 1), 0.0, tap))
            term = tap * pltpu.roll(tapped, lax.rem(col_at + (BREADTH + t - 1), BREADTH), 1)
            wide_all = term if t == 0 else wide_all + term
            begun = tall(line >= col_at + (t - 1))
            wide_low = jnp.where(begun, wide_all, 0.0 if t == 0 else wide_low)
        wide_high = wide_all - wide_low
        low, high = sums[2 * (q % 2)], sums[2 * (q % 2) + 1]
        low[pl.ds(row_at + 7, WINDOW), :] += wide_low
        high[pl.ds(row_at + 7, WINDOW), :] += wide_high

    used = OUTER * HEIGHT
    still = pl.ds((OUTER // 2) * HEIGHT, HEIGHT)
    for ref in (shifted_a, shifted_b):
        ref[:, used:, :] = jnp.zeros((GROUP, PATCH - used, PATCH), BF16)
        ref[:, still, BREADTH:] = jnp.zeros((GROUP, HEIGHT, BREADTH), BF16)
    def note(s, carry):
        number, empty = carry
        holds = whole_s[2, s]
        listed[number] = s
        return number + holds, jnp.where(holds == 0, s, empty)

    number, empty = lax.fori_loop(0, slots, note, (0, 0), unroll=16)

    def fill(n, carry):
        listed[number + n] = empty
        return carry

    lax.fori_loop(0, 2 * GROUP, fill, 0, unroll=4)
    rounds = jnp.maximum((number + 2 * GROUP - 1) // (2 * GROUP), 1)
    groups = 2 * rounds
    for q in range(GROUP):
        build(0, q, left_a, shifted_a)

    def work(h, carry):
        g = 2 * h
        for q in range(GROUP):
            convolve(q, left_a, shifted_a, padded_a)
            build(g + 1, q, left_b, shifted_b)
            resample(jnp.maximum(g - 1, 0), q, padded_b)
        for q in range(GROUP):
            convolve(q, left_b, shifted_b, padded_b)
            build(jnp.minimum(g + 2, groups - 1), q, left_a, shifted_a)
            resample(g, q, padded_a)
        return carry

    lax.fori_loop(0, rounds, work, 0)
    for q in range(GROUP):
        resample(groups - 1, q, padded_b)
    for v in range(shares):
        rows = pl.ds(8 + v * HEIGHT, HEIGHT)
        for half in range(2):
            both = sums[half][rows, :] + sums[2 + half][rows, :]
            out[v, :HEIGHT, half * BREADTH : (half + 1) * BREADTH] = both.astype(out.dtype)


def coadd_sums(blocks):
    sources = blocks.shape[0]
    slots = CAP * sources
    vmem = pl.BlockSpec(memory_space=pltpu.VMEM)
    return pl.pallas_call(
        functools.partial(coadd_body, sources),
        out_shape=jax.ShapeDtypeStruct((PATCH // HEIGHT, 2 * HEIGHT, PATCH), BF16),
        in_specs=[vmem],
        out_specs=vmem,
        scratch_shapes=[
            pltpu.VMEM((sources * TAIL, BREADTH), F32),
            pltpu.VMEM((slots, BREADTH), F32),
            pltpu.VMEM((2 * INNER, slots, BREADTH), F32),
            pltpu.VMEM((GROUP, INNER * HEIGHT, PATCH), BF16),
            pltpu.VMEM((GROUP, INNER * HEIGHT, PATCH), BF16),
            pltpu.VMEM((GROUP, PATCH, PATCH), BF16),
            pltpu.VMEM((GROUP, PATCH, PATCH), BF16),
            pltpu.VMEM((GROUP, 8 + HEIGHT + 8, BREADTH), F32),
            pltpu.VMEM((GROUP, 8 + HEIGHT + 8, BREADTH), F32),
            pltpu.VMEM((PATCH + 16, BREADTH), F32),
            pltpu.VMEM((PATCH + 16, BREADTH), F32),
            pltpu.VMEM((PATCH + 16, BREADTH), F32),
            pltpu.VMEM((PATCH + 16, BREADTH), F32),
            pltpu.VMEM((8, slots), F32),
            pltpu.VMEM((8, slots), jnp.int32),
            pltpu.SMEM((8, slots), F32),
            pltpu.SMEM((8, slots), jnp.int32),
            pltpu.SMEM((slots + 2 * GROUP,), jnp.int32),
            pltpu.SemaphoreType.DMA((2,)),
        ],
        compiler_params=pltpu.CompilerParams(vmem_limit_bytes=48 << 20),
        name="coadd",
    )(blocks)


def finish_body(sums, coadd, depth_map):
    total = sums[0].astype(F32)
    for v in range(1, sums.shape[0]):
        total = total + sums[v].astype(F32)
    depth = total[HEIGHT:, :]
    depth_map[...] = depth
    coadd[...] = total[:HEIGHT, :] / (1.0 + depth)


def finish(sums):
    vmem = pl.BlockSpec(memory_space=pltpu.VMEM)
    return pl.pallas_call(
        finish_body,
        out_shape=[jax.ShapeDtypeStruct((HEIGHT, PATCH), F32)] * 2,
        in_specs=[vmem],
        out_specs=[vmem, vmem],
        compiler_params=pltpu.CompilerParams(vmem_limit_bytes=4 << 20),
        name="finish",
    )(sums)


def per_device(stamps, coefs, basis, taps, weights, target, row_offset, col_offset):
    places = lax.axis_size("patch")
    blocks = pack(
        target[:, :, 0], stamps[0], coefs[0].T, basis[0, 0], taps[0].T, weights, row_offset, col_offset, places
    )
    blocks = lax.all_to_all(blocks, "patch", split_axis=0, concat_axis=0, tiled=True)
    sums = coadd_sums(blocks)
    sums = lax.all_to_all(sums, "visit", split_axis=0, concat_axis=0, tiled=True)
    coadd, depth_map = finish(sums)
    return (coadd[None], depth_map[None])


def solution(mesh):
    placed = (
        P("visit", "patch", None, None),
        P("visit", "patch", None),
        P("visit", "patch", None, None),
        P("visit", "patch", None),
        P("visit", "patch"),
        P("visit", "patch", None),
        P("visit", "patch"),
        P("visit", "patch"),
    )
    return jax.shard_map(
        per_device,
        mesh=mesh,
        in_specs=placed,
        out_specs=(P("patch", "visit", None), P("patch", "visit", None)),
        check_vma=False,
    )
```
